32 devices in a mesh: rows: 8 (over z, x), ch: 4 (over y, core).
Axes of the slice: x: 2, y: 2, z: 4, core: 2. Of those that a mesh axis runs over, the one named last changes fastest.
Arguments:
- features: bfloat16 [64, 4096], P('ch', 'rows'), may hold values from -6 to 6
- tiles: bfloat16 [32, 20, 128, 128], P('rows'), may hold values from -0.0625 to 0.0625
- tile_cols: int32 [32, 20], P('rows'), may hold values from 0 to 11, as said below
- needs: int32 [8, 8, 1], P('rows'), may hold values from -1 to 3, as said below
- weights: bfloat16 [4, 64, 64], P(None, 'ch'), may hold values from -0.375 to 0.375
- cotangent: bfloat16 [64, 4096], P('ch', 'rows'), may hold values from -6 to 6
Outputs:
- output: bfloat16 [64, 4096], P('ch', 'rows')
- feature_grad: bfloat16 [64, 4096], P('ch', 'rows')
- weight_grad: float32 [4, 64, 64], P(None, 'ch')
The draws below stay inside these ranges and needn't reach their ends.
Inputs may be any that keep to these rules, and one draw needn't show every extreme that they name: needs[d, o, s] is a block index of device o, or -1 where unset; row o = d is unset; slot 0 is set for every o other than d; the set entries of one (d, o) differ; some device o has all 1 slots set by every other device. `tile_cols`: the first tile of row block b is its own block (entry b mod 4); an entry v >= 4 names cell v - 4 = 1 o + s with needs[d, o, s] set; every set entry of needs[d] is named by some tile of device d.
All inputs are finite; a program needn't handle non-finite values.
Results may differ from the reference program's by a relative error of at most 0.0055.
Values may be sent and summed in bfloat16 or wider, within the bound.
No kernel may reach another device: no remote copies, remote signals or barrier semaphores. Data moves between devices by JAX's collectives and lax.ppermute only.
A program may use at most 64 MiB of HBM per device.

```python
import jax
import jax.numpy as jnp
from jax import lax

C = 64
CO = 64
K = 4
BLK = 128
TPR = 20
SLOT = 1
NB_DEV = 4
SHARDS = 8
NBLK = 32
NODES = 4096


def shared_layout(key):
    base = jax.random.fold_in(key, 11)
    key_hub, key_order, key_second, key_place, key_local = jax.random.split(base, 5)
    hub_device = jax.random.randint(key_hub, (), 0, SHARDS)
    scores = jax.random.randint(key_order, (SHARDS, SHARDS, NB_DEV), 0, 1 << 20) * NB_DEV + jnp.arange(NB_DEV, dtype=jnp.int32)
    chosen = jnp.argsort(scores, axis=-1)[..., :SLOT].astype(jnp.int32)
    device = jnp.arange(SHARDS, dtype=jnp.int32)[:, None]
    holder = jnp.arange(SHARDS, dtype=jnp.int32)[None, :]
    first_set = device != holder
    coin = jax.random.randint(key_second, (SHARDS, SHARDS), 0, 2) == 1
    later_set = first_set & (coin | (holder == hub_device))
    slot_index = jnp.arange(SLOT, dtype=jnp.int32)
    set_mask = first_set[..., None] & ((slot_index == 0) | later_set[..., None])
    needs = jnp.where(set_mask, chosen, -1).astype(jnp.int32)
    spots = NB_DEV * (TPR - 1)
    place_scores = jax.random.randint(key_place, (SHARDS, spots), 0, 1 << 20) * spots + jnp.arange(spots, dtype=jnp.int32)
    place = jnp.argsort(place_scores, axis=-1).astype(jnp.int32)
    cell_valid = place < SHARDS * SLOT
    ghost_cell = jnp.minimum(place, SHARDS * SLOT - 1)
    flat_needs = needs.reshape(SHARDS, SHARDS * SLOT)
    cell_used = jnp.take_along_axis(flat_needs, ghost_cell, axis=1) >= 0
    local_pick = jax.random.randint(key_local, (SHARDS, spots), 0, NB_DEV)
    others = jnp.where(cell_valid & cell_used, NB_DEV + ghost_cell, local_pick).reshape(SHARDS, NB_DEV, TPR - 1)
    diagonal = jnp.broadcast_to(jnp.arange(NB_DEV, dtype=jnp.int32)[None, :, None], (SHARDS, NB_DEV, 1))
    tile_cols = jnp.concatenate([diagonal, others.astype(jnp.int32)], axis=-1).reshape(NBLK, TPR)
    return (needs, tile_cols)


def draw_needs(key, part):
    return shared_layout(key)[0].astype(jnp.int32)


def draw_tile_cols(key, part):
    return shared_layout(key)[1].astype(jnp.int32)


def shard_levels(rng, shape, cuts, least, top_value):
    level = 1.0
    for axis_at, shards_of in cuts:
        heights = jax.random.uniform(jax.random.fold_in(jax.random.fold_in(rng, 6), axis_at), (shards_of,), jnp.float32, least / len(cuts), top_value / len(cuts))
        level = level * jnp.repeat(jnp.exp(heights), shape[axis_at] // shards_of).reshape((-1,) + (1,) * (len(shape) - 1 - axis_at))
    return level


def gaussian(stream_key, extent, width, most, shards=(), kind=jnp.bfloat16):
    result = jax.random.normal(stream_key, extent, jnp.float32) * width
    if len(shards) > 0:
        result = shard_levels(stream_key, extent, shards, -0.22, 0.18) * result
    return jnp.clip(result, min=-most, max=most).astype(kind)


def setup_inputs(seed: int = 0) -> dict:
    arg_keys = jax.random.split(jax.random.key(seed), 7)
    features = gaussian(arg_keys[0], (C, NODES), 1.0, 6.0, ((0, 4), (1, 8)))
    tiles = gaussian(arg_keys[1], (NBLK, TPR, BLK, BLK), (4 * TPR * BLK) ** -0.5, 0.0625, ((0, 8),))
    tile_cols = draw_tile_cols(jax.random.fold_in(arg_keys[6], 71), 0)
    needs = draw_needs(jax.random.fold_in(arg_keys[6], 71), 0)
    weights = gaussian(arg_keys[4], (K, C, CO), (K * C) ** -0.5, 0.375, ((1, 4),))
    cotangent = gaussian(arg_keys[5], (CO, NODES), 1.0, 6.0, ((0, 4), (1, 8)))
    return dict(features=features, tiles=tiles, tile_cols=tile_cols, needs=needs, weights=weights, cotangent=cotangent)


def to_half(value):
    return lax.optimization_barrier(value.astype(jnp.bfloat16))


def resolve_columns(tile_cols, needs):
    device = (jnp.arange(NBLK, dtype=jnp.int32) // NB_DEV).astype(jnp.int32)
    ghost_cell = jnp.clip(tile_cols - NB_DEV, 0, SHARDS * SLOT - 1).astype(jnp.int32)
    holder = ghost_cell // SLOT
    flat_needs = needs.reshape(SHARDS, SHARDS * SLOT)[device]
    needed = jnp.take_along_axis(flat_needs, ghost_cell, axis=1)
    remote = holder * NB_DEV + jnp.maximum(needed, 0)
    local = device[:, None] * NB_DEV + tile_cols
    return jnp.where(tile_cols < NB_DEV, local, remote).astype(jnp.int32)


def apply_op(value, tiles, columns):
    blocked = value.astype(jnp.float32).reshape(C, NBLK, BLK)

    def group(index):
        row_cols = lax.dynamic_slice_in_dim(columns, index * NB_DEV, NB_DEV, 0)
        tile_group = lax.dynamic_slice_in_dim(tiles, index * NB_DEV, NB_DEV, 0).astype(jnp.float32)
        source = blocked[:, row_cols.reshape(-1), :].reshape(C, NB_DEV, TPR, BLK)
        return jnp.einsum('crtj,rtij->cri', source, tile_group)

    pieces = lax.map(group, jnp.arange(SHARDS, dtype=jnp.int32))
    return pieces.transpose(1, 0, 2, 3).reshape(C, NODES)


def apply_transposed(value, tiles, columns):
    blocked = value.astype(jnp.float32).reshape(C, NBLK, BLK)

    def accumulate(total, index):
        row_cols = lax.dynamic_slice_in_dim(columns, index * NB_DEV, NB_DEV, 0)
        tile_group = lax.dynamic_slice_in_dim(tiles, index * NB_DEV, NB_DEV, 0).astype(jnp.float32)
        segment = lax.dynamic_slice_in_dim(blocked, index * NB_DEV, NB_DEV, 1)
        contrib = jnp.einsum('cri,rtij->crtj', segment, tile_group).reshape(C, NB_DEV * TPR, BLK)
        return total.at[:, row_cols.reshape(-1), :].add(contrib), None

    total, _ = lax.scan(accumulate, jnp.zeros((C, NBLK, BLK), jnp.float32), jnp.arange(SHARDS, dtype=jnp.int32))
    return total.reshape(C, NODES)


def reference(features, tiles, tile_cols, needs, weights, cotangent):
    columns = resolve_columns(tile_cols, needs)
    cheb_terms = [features, to_half(apply_op(features, tiles, columns))]
    for degree in range(2, K):
        latest = 2.0 * apply_op(cheb_terms[-1], tiles, columns) - cheb_terms[-2].astype(jnp.float32)
        cheb_terms.append(to_half(latest))
    stacked = jnp.stack(cheb_terms).astype(jnp.float32)
    weight_f = weights.astype(jnp.float32)
    grad_out = cotangent.astype(jnp.float32)
    output = jnp.einsum('kio,kin->on', weight_f, stacked).astype(jnp.bfloat16)
    weight_grad = jnp.einsum('kin,on->kio', stacked, grad_out)
    term_grads = jnp.einsum('kio,on->kin', weight_f, grad_out)
    adjoints = [term_grads[degree] for degree in range(K)]
    for degree in range(K - 1, 1, -1):
        rounded = to_half(adjoints[degree])
        adjoints[degree - 1] = adjoints[degree - 1] + 2.0 * apply_transposed(rounded, tiles, columns)
        adjoints[degree - 2] = adjoints[degree - 2] - adjoints[degree]
    last = apply_transposed(to_half(adjoints[1]), tiles, columns)
    feature_grad = (adjoints[0] + last).astype(jnp.bfloat16)
    return output, feature_grad, weight_grad
```

```python
import functools

import jax
import jax.numpy as jnp
from jax import lax
from jax.experimental import pallas as pl
from jax.experimental.pallas import tpu as pltpu
from jax.sharding import PartitionSpec as P

K = 4
BF = jnp.bfloat16
F32 = jnp.float32
SMEM = pltpu.MemorySpace.SMEM
VMEM = pltpu.MemorySpace.VMEM


def nn(a, b):
    return lax.dot_general(a, b, (((1,), (0,)), ((), ())), preferred_element_type=F32)


def nt(a, b):
    return lax.dot_general(a, b, (((1,), (1,)), ((), ())), preferred_element_type=F32)


def lanes(index, width):
    return pl.ds(pl.multiple_of(index * width, width), width)


def push_kernel(cols, needs, f, c, w, tiles, x1, pack, cells, where, buf, acc, sems):
    nb, tpr = cols.shape
    n, ci, bw = acc.shape

    def scan(i, count):
        r = i // (tpr - 1)
        t = i % (tpr - 1) + 1
        v = cols[r, t]
        ghost = v >= nb

        @pl.when(ghost)
        def _():
            cells[count] = v - nb
            where[count] = r
            pltpu.make_async_copy(tiles.at[r, t], buf.at[count], sems.at[count]).start()

        return count + ghost.astype(jnp.int32)

    count = lax.fori_loop(0, nb * (tpr - 1), scan, 0)
    for o in range(n):
        acc[o] = jnp.zeros((ci, bw), F32)
        for b in range(nb):
            x1[o, b * ci : (b + 1) * ci, :] = f[:, b * bw : (b + 1) * bw]
        x1[o, (nb + 1) * ci :, :] = jnp.full((ci, bw), needs[0, o, 0].astype(F32)).astype(BF)
    pack[0:ci] = f[...]
    pack[ci : 2 * ci] = c[...]
    for k in range(K):
        width = w.shape[2]
        pack[2 * ci :, k * width : (k + 1) * width] = w[k]

    def product(i, carry):
        pltpu.make_async_copy(tiles.at[0, 0], buf.at[i], sems.at[i]).wait()
        o = cells[i]
        acc[o] += nn(c[:, lanes(where[i], bw)], buf[i])
        return carry

    lax.fori_loop(0, count, product, 0)
    for o in range(n):
        x1[o, nb * ci : (nb + 1) * ci, :] = acc[o].astype(BF)


def combine_kernel(cols, f, c, tiles, op, lf, ltc, total):
    r = pl.program_id(0)
    tpr = tiles.shape[1]
    bw = tiles.shape[2]
    own = f.shape[1]
    total[...] = jnp.zeros_like(total)
    for t in range(tpr):
        at = lanes(cols[r, t], bw)
        total[:, at] += tiles[0, t].astype(F32)
    op[...] = total[...].astype(BF)
    local = op[:, :own]
    lf[...] = nt(f[...], local)
    part = nn(c[:, lanes(r, bw)], local)

    @pl.when(r == 0)
    def _():
        ltc[...] = part

    @pl.when(r > 0)
    def _():
        ltc[...] += part


def first_kernel(needs, y1, op, lf, ltc, x2, tu, marks_ref, gh):
    n, rows, bw = y1.shape
    ci, own = lf.shape
    nb = own // bw
    q = x2.shape[0] // n
    for o in range(n):
        at = jnp.maximum(needs[0, o, 0], 0) * ci
        gh[:, o * bw : (o + 1) * bw] = y1[o, pl.ds(pl.multiple_of(at, ci), ci), :]
    t1 = (lf[...] + nt(gh[...], op[:, own:])).astype(BF)
    marks = [y1[o, (nb + 1) * ci :, :].astype(F32) for o in range(n)]
    for o in range(n):
        marks_ref[o] = y1[o, (nb + 1) * ci :, :]
    u1 = []
    for b in range(nb):
        u = ltc[:, b * bw : (b + 1) * bw]
        for o in range(n):
            u = u + jnp.where(marks[o] == b, y1[o, nb * ci : (nb + 1) * ci, :].astype(F32), 0.0)
        u1.append(u.astype(BF))
    tu[0:ci] = t1
    for b in range(nb):
        tu[ci:, b * bw : (b + 1) * bw] = u1[b]
    sent = nn(tu[ci:], op[:, own:]).astype(BF)
    tf = t1.astype(F32)
    for o in range(n):
        blk = jnp.zeros((ci, bw), F32)
        for b in range(nb):
            blk = jnp.where(marks[o] == b, tf[:, b * bw : (b + 1) * bw], blk)
        blk = blk.astype(BF)
        for s in range(q):
            x2[o * q + s, 0:ci, :] = blk
            x2[o * q + s, ci:, :] = sent[:, o * bw : (o + 1) * bw]


def gather_kernel(q, refs):
    packs = refs[:q]
    tus = refs[q : 2 * q]
    op, tpre, upre, full, wt, wg, wbuf = refs[2 * q :]
    own = tpre.shape[1]
    total = tpre.shape[0]
    ci = total // q
    co = wt.shape[1]
    me = lax.axis_index("ch")
    for s in range(q):
        at = lax.rem(me - s + q, q) * ci
        spot = pl.ds(pl.multiple_of(at, ci), ci)
        full[0, spot, :] = packs[s][0:ci, :]
        full[1, spot, :] = packs[s][ci : 2 * ci, :]
        full[2, spot, :] = tus[s][0:ci, :]
        full[3, spot, :] = tus[s][ci:, :]
        wbuf[spot, :] = packs[s][2 * ci :, : K * co].astype(F32)
    for k in range(K):
        turned = wbuf[:, k * co : (k + 1) * co].T
        wt[k] = turned.astype(BF)
    local = op[:, :own]
    tpre[...] = 2.0 * nt(full[2], local) - full[0].astype(F32)
    upre[...] = 2.0 * nn(full[3], local) - full[1].astype(F32)
    wg[0] = nt(packs[0][0:ci, :], full[1])
    wg[1] = nt(tus[0][0:ci, :], full[1])


def second_kernel(q, y2, marks_ref, op, tpre, upre, full, wt, wg, w, x3, two, gh2, gh, low):
    n, ci, bw = marks_ref.shape
    total, own = tpre.shape
    nb = own // bw
    me = lax.axis_index("ch")
    mine = pl.ds(pl.multiple_of(me * ci, ci), ci)
    for o in range(n):
        for s in range(q):
            gh[s * ci : (s + 1) * ci, o * bw : (o + 1) * bw] = y2[o * q + s, 0:ci, :]
    two[0] = (tpre[...] + 2.0 * nt(gh[...], op[:, own:])).astype(BF)
    marks = [marks_ref[o].astype(F32) for o in range(n)]
    for s in range(q):
        for b in range(nb):
            u = jnp.zeros((ci, bw), F32)
            for o in range(n):
                u = u + jnp.where(marks[o] == b, y2[o * q + s, ci:, :].astype(F32), 0.0)
            spot = (slice(s * ci, (s + 1) * ci), slice(b * bw, (b + 1) * bw))
            two[(1,) + spot] = (upre[spot] + 2.0 * u).astype(BF)
    g = nn(wt[K - 1, mine, :], two[0]).astype(BF)
    h = nn(w[K - 1], two[1]).astype(BF)
    gh2[0] = g
    gh2[1] = h
    sent = nn(h, op[:, own:]).astype(BF)
    t2 = two[0, mine, :]
    co = w.shape[2]
    wg2 = nt(t2, full[1])
    wg3 = 2.0 * nt(t2, full[3]) - wg[1]
    low[0:ci, 0:co] = wg[0]
    low[0:ci, co:] = wg[1]
    low[ci:, 0:co] = wg2
    low[ci:, co:] = wg3
    packed = low[...].astype(BF)
    gf = g.astype(F32)
    for o in range(n):
        blk = jnp.zeros((ci, bw), F32)
        for b in range(nb):
            blk = jnp.where(marks[o] == b, gf[:, b * bw : (b + 1) * bw], blk)
        x3[o, 0:ci, :] = blk.astype(BF)
        x3[o, ci : 2 * ci, :] = sent[:, o * bw : (o + 1) * bw]
        x3[o, 2 * ci :, :] = packed


def local_kernel(op, full, two, gh2, wt, w, outl, fgl):
    ci, own = outl.shape
    me = lax.axis_index("ch")
    mine = pl.ds(pl.multiple_of(me * ci, ci), ci)
    local = op[:, :own]
    out = nn(wt[0, mine, :], full[0]) + nn(wt[1, mine, :], full[2]) - nn(wt[3, mine, :], full[2])
    outl[...] = out + nn(wt[2, mine, :], two[0]) + 2.0 * nt(gh2[0], local)
    fg = nn(w[0], full[1]) + nn(w[1], full[3]) - nn(w[3], full[3])
    fgl[...] = fg + nn(w[2], two[1]) + 2.0 * nn(gh2[1], local)


def last_kernel(y3, marks_ref, op, outl, fgl, out, fg, wgrad, gh):
    n, ci, bw = marks_ref.shape
    own = outl.shape[1]
    nb = own // bw
    co = wgrad.shape[2]
    for o in range(n):
        gh[:, o * bw : (o + 1) * bw] = y3[o, 0:ci, :]
    out[...] = (outl[...] + 2.0 * nt(gh[...], op[:, own:])).astype(BF)
    for b in range(nb):
        u = jnp.zeros((ci, bw), F32)
        for o in range(n):
            u = u + jnp.where(marks_ref[o].astype(F32) == b, y3[o, ci : 2 * ci, :].astype(F32), 0.0)
        spot = slice(b * bw, (b + 1) * bw)
        fg[:, spot] = (fgl[:, spot] + 2.0 * u).astype(BF)
    wsum = y3[0, 2 * ci :, :].astype(F32)
    for o in range(1, n):
        wsum = wsum + y3[o, 2 * ci :, :].astype(F32)
    wgrad[0] = wsum[0:ci, 0:co]
    wgrad[1] = wsum[0:ci, co:]
    wgrad[2] = wsum[ci:, 0:co]
    wgrad[3] = wsum[ci:, co:]


def body(features, tiles, tile_cols, needs, weights, cotangent):
    ci, own = features.shape
    nb, tpr, bw, _ = tiles.shape
    co = weights.shape[2]
    n = lax.axis_size("rows")
    q = lax.axis_size("ch")
    total = ci * q
    cells = nb + n
    wide = cells * bw
    struct = jax.ShapeDtypeStruct
    smem = pl.BlockSpec(memory_space=SMEM)
    vmem = pl.BlockSpec(memory_space=VMEM)
    limit = (16 << 20) + 4 * own * wide * 2
    params = pltpu.CompilerParams(vmem_limit_bytes=limit)

    x1, pack = pl.pallas_call(
        push_kernel,
        out_shape=(struct((n, (nb + 2) * ci, bw), BF), struct((3 * ci, own), BF)),
        in_specs=[smem, smem, vmem, vmem, vmem, pl.BlockSpec(memory_space=pl.ANY)],
        out_specs=(vmem, vmem),
        scratch_shapes=[
            pltpu.SMEM((nb * tpr,), jnp.int32),
            pltpu.SMEM((nb * tpr,), jnp.int32),
            pltpu.VMEM((nb * tpr, bw, bw), BF),
            pltpu.VMEM((n, ci, bw), F32),
            pltpu.SemaphoreType.DMA((nb * tpr,)),
        ],
        compiler_params=params,
        name="push",
    )(tile_cols, needs, features, cotangent, weights, tiles)
    y1 = lax.all_to_all(x1, "rows", 0, 0)

    op, lf, ltc = pl.pallas_call(
        combine_kernel,
        grid=(nb,),
        out_shape=(struct((own, wide), BF), struct((ci, own), F32), struct((ci, own), F32)),
        in_specs=[
            smem,
            pl.BlockSpec((ci, own), lambda r: (0, 0)),
            pl.BlockSpec((ci, own), lambda r: (0, 0)),
            pl.BlockSpec((1, tpr, bw, bw), lambda r: (r, 0, 0, 0)),
        ],
        out_specs=(
            pl.BlockSpec((bw, wide), lambda r: (r, 0)),
            pl.BlockSpec((ci, bw), lambda r: (0, r)),
            pl.BlockSpec((ci, own), lambda r: (0, 0)),
        ),
        scratch_shapes=[pltpu.VMEM((bw, wide), F32)],
        compiler_params=params,
        cost_estimate=pl.CostEstimate(flops=4 * ci * own * own, bytes_accessed=8 << 20, transcendentals=0),
        name="combine",
    )(tile_cols, features, cotangent, tiles)

    def around(value):
        moved = [value]
        for s in range(1, q):
            moved.append(lax.ppermute(value, "ch", [(i, (i + s) % q) for i in range(q)]))
        return moved

    packs = around(pack)

    x2, tu, marks = pl.pallas_call(
        first_kernel,
        out_shape=(struct((n * q, 2 * ci, bw), BF), struct((2 * ci, own), BF), struct((n, ci, bw), BF)),
        in_specs=[smem, vmem, vmem, vmem, vmem],
        out_specs=(vmem,) * 3,
        scratch_shapes=[pltpu.VMEM((ci, n * bw), BF)],
        compiler_params=params,
        name="first",
    )(needs, y1, op, lf, ltc)
    y2 = lax.all_to_all(x2, ("rows", "ch"), 0, 0)
    tus = around(tu)

    tpre, upre, full, wt, wg = pl.pallas_call(
        lambda *refs: gather_kernel(q, refs),
        out_shape=(
            struct((total, own), F32),
            struct((total, own), F32),
            struct((4, total, own), BF),
            struct((K, co, total), BF),
            struct((2, ci, co), F32),
        ),
        in_specs=[vmem] * (2 * q + 1),
        out_specs=(vmem,) * 5,
        scratch_shapes=[pltpu.VMEM((total, K * co), F32)],
        compiler_params=params,
        cost_estimate=pl.CostEstimate(flops=4 * total * own * own, bytes_accessed=4 << 20, transcendentals=0),
        name="gather",
    )(*packs, *tus, op)

    x3, two, gh2 = pl.pallas_call(
        functools.partial(second_kernel, q),
        out_shape=(struct((n, 4 * ci, bw), BF), struct((2, total, own), BF), struct((2, ci, own), BF)),
        in_specs=[vmem] * 9,
        out_specs=(vmem,) * 3,
        scratch_shapes=[pltpu.VMEM((total, n * bw), BF), pltpu.VMEM((2 * ci, bw), F32)],
        compiler_params=params,
        name="second",
    )(y2, marks, op, tpre, upre, full, wt, wg, weights)
    y3 = lax.all_to_all(x3, "rows", 0, 0)

    outl, fgl = pl.pallas_call(
        local_kernel,
        out_shape=(struct((ci, own), F32), struct((ci, own), F32)),
        in_specs=[vmem] * 6,
        out_specs=(vmem,) * 2,
        compiler_params=params,
        cost_estimate=pl.CostEstimate(flops=8 * total * ci * own, bytes_accessed=4 << 20, transcendentals=0),
        name="local",
    )(op, full, two, gh2, wt, weights)

    output, feature_grad, weight_grad = pl.pallas_call(
        last_kernel,
        out_shape=(struct((ci, own), BF), struct((ci, own), BF), struct((K, ci, co), F32)),
        in_specs=[vmem] * 5,
        out_specs=(vmem,) * 3,
        scratch_shapes=[pltpu.VMEM((ci, n * bw), BF)],
        compiler_params=params,
        name="last",
    )(y3, marks, op, outl, fgl)
    return output, feature_grad, weight_grad


def solution(mesh):
    placed = (
        P("ch", "rows"),
        P("rows", None, None, None),
        P("rows", None),
        P("rows", None, None),
        P(None, "ch", None),
        P("ch", "rows"),
    )
    return jax.shard_map(
        body,
        mesh=mesh,
        in_specs=placed,
        out_specs=(P("ch", "rows"), P("ch", "rows"), P(None, "ch", None)),
        check_vma=False,
    )
```

```python
import functools

import jax
import jax.numpy as jnp
from jax import lax
from jax.experimental import pallas as pl
from jax.experimental.pallas import tpu as pltpu
from jax.sharding import PartitionSpec as P

K = 4
BF = jnp.bfloat16
F32 = jnp.float32
SMEM = pltpu.MemorySpace.SMEM
VMEM = pltpu.MemorySpace.VMEM


def nn(a, b):
    return lax.dot_general(a, b, (((1,), (0,)), ((), ())), preferred_element_type=F32)


def nt(a, b):
    return lax.dot_general(a, b, (((1,), (1,)), ((), ())), preferred_element_type=F32)


def lanes(index, width):
    return pl.ds(pl.multiple_of(index * width, width), width)


def push_kernel(cols_h, needs_h, f_h, c_h, w_h, tiles, x1, pack, cols, needs, cells, where, f, c, w, buf, acc, sems):
    nb, tpr = cols.shape
    n, ci, bw = acc.shape
    small = [(cols_h, cols), (needs_h, needs), (f_h, f), (c_h, c), (w_h, w)]
    copies = [pltpu.make_async_copy(src, dst, sems.at[i]) for i, (src, dst) in enumerate(small)]
    for r in range(nb):
        copies.append(pltpu.make_async_copy(tiles.at[r], buf.at[pl.ds(r * tpr, tpr)], sems.at[len(small) + r]))
    for copy in copies:
        copy.start()
    for o in range(n):
        acc[o] = jnp.zeros((ci, bw), F32)
    copies[0].wait()
    count = jnp.int32(0)
    for r in range(nb):
        for t in range(1, tpr):
            v = cols[r, t]
            cells[count] = v - nb
            where[count] = r * tpr + t
            count = count + (v >= nb).astype(jnp.int32)
    for copy in copies[1:5]:
        copy.wait()
    for o in range(n):
        for b in range(nb):
            x1[o, b * ci : (b + 1) * ci, :] = f[:, b * bw : (b + 1) * bw]
        x1[o, (nb + 1) * ci :, :] = jnp.full((ci, bw), needs[0, o].astype(F32)).astype(BF)
    pack[0:ci] = f[...]
    pack[ci : 2 * ci] = c[...]
    for k in range(K):
        width = w.shape[2]
        pack[2 * ci :, k * width : (k + 1) * width] = w[k]
    for copy in copies[5:]:
        copy.wait()

    def products(step, carry):
        for j in range(n):
            i = jnp.minimum(step * n + j, nb * tpr - 1)
            live = i < count
            o = jnp.where(live, cells[i], 0)
            at = jnp.where(live, where[i], 0)
            part = nn(c[:, lanes(at // tpr, bw)], buf[at])
            acc[o] += jnp.where(live, part, 0.0)
        return carry

    lax.fori_loop(0, (count + n - 1) // n, products, 0)
    for o in range(n):
        x1[o, nb * ci : (nb + 1) * ci, :] = acc[o].astype(BF)


def combine_kernel(cols, f, c, tiles, op, lf, ltc, total, buf, sems):
    nb, tpr = cols.shape
    bw = tiles.shape[2]
    own = f.shape[1]
    copies = [pltpu.make_async_copy(tiles.at[r], buf.at[r], sems.at[r]) for r in range(nb)]
    for copy in copies:
        copy.start()
    for r in range(nb):
        rows = slice(r * bw, (r + 1) * bw)
        total[...] = jnp.zeros_like(total)
        copies[r].wait()
        for t in range(tpr):
            at = lanes(cols[r, t], bw)
            total[:, at] += buf[r, t].astype(F32)
        op[rows, :] = total[...].astype(BF)
    local = op[:, :own]
    lf[...] = nt(f[...], local)
    ltc[...] = nn(c[...], local)


def first_kernel(needs, y1, op, lf, ltc, x2, tu, marks_ref, gh):
    n, rows, bw = y1.shape
    ci, own = lf.shape
    nb = own // bw
    q = x2.shape[0] // n
    for o in range(n):
        at = jnp.maximum(needs[0, o], 0) * ci
        gh[:, o * bw : (o + 1) * bw] = y1[o, pl.ds(pl.multiple_of(at, ci), ci), :]
    t1 = (lf[...] + nt(gh[...], op[:, own:])).astype(BF)
    marks = [y1[o, (nb + 1) * ci :, :].astype(F32) for o in range(n)]
    for o in range(n):
        marks_ref[o] = y1[o, (nb + 1) * ci :, :]
    u1 = []
    for b in range(nb):
        u = ltc[:, b * bw : (b + 1) * bw]
        for o in range(n):
            u = u + jnp.where(marks[o] == b, y1[o, nb * ci : (nb + 1) * ci, :].astype(F32), 0.0)
        u1.append(u.astype(BF))
    tu[0:ci] = t1
    for b in range(nb):
        tu[ci:, b * bw : (b + 1) * bw] = u1[b]
    sent = nn(tu[ci:], op[:, own:]).astype(BF)
    tf = t1.astype(F32)
    for o in range(n):
        blk = jnp.zeros((ci, bw), F32)
        for b in range(nb):
            blk = jnp.where(marks[o] == b, tf[:, b * bw : (b + 1) * bw], blk)
        blk = blk.astype(BF)
        for s in range(q):
            x2[o * q + s, 0:ci, :] = blk
            x2[o * q + s, ci:, :] = sent[:, o * bw : (o + 1) * bw]


def gather_kernel(q, refs):
    packs = refs[:q]
    tus = refs[q : 2 * q]
    op, tpre, upre, full, wt, wg, wbuf = refs[2 * q :]
    own = tpre.shape[1]
    total = tpre.shape[0]
    ci = total // q
    co = wt.shape[1]
    me = lax.axis_index("ch")
    for s in range(q):
        at = lax.rem(me - s + q, q) * ci
        spot = pl.ds(pl.multiple_of(at, ci), ci)
        full[0, spot, :] = packs[s][0:ci, :]
        full[1, spot, :] = packs[s][ci : 2 * ci, :]
        full[2, spot, :] = tus[s][0:ci, :]
        full[3, spot, :] = tus[s][ci:, :]
        wbuf[spot, :] = packs[s][2 * ci :, : K * co].astype(F32)
    for k in range(K):
        turned = wbuf[:, k * co : (k + 1) * co].T
        wt[k] = turned.astype(BF)
    local = op[:, :own]
    tpre[...] = 2.0 * nt(full[2], local) - full[0].astype(F32)
    upre[...] = 2.0 * nn(full[3], local) - full[1].astype(F32)
    wg[0] = nt(packs[0][0:ci, :], full[1])
    wg[1] = nt(tus[0][0:ci, :], full[1])


def second_kernel(q, y2, marks_ref, op, tpre, upre, full, wt, wg, w, x3, two, gh2, gh, low):
    n, ci, bw = marks_ref.shape
    total, own = tpre.shape
    nb = own // bw
    me = lax.axis_index("ch")
    mine = pl.ds(pl.multiple_of(me * ci, ci), ci)
    for o in range(n):
        for s in range(q):
            gh[s * ci : (s + 1) * ci, o * bw : (o + 1) * bw] = y2[o * q + s, 0:ci, :]
    two[0] = (tpre[...] + 2.0 * nt(gh[...], op[:, own:])).astype(BF)
    marks = [marks_ref[o].astype(F32) for o in range(n)]
    for s in range(q):
        for b in range(nb):
            u = jnp.zeros((ci, bw), F32)
            for o in range(n):
                u = u + jnp.where(marks[o] == b, y2[o * q + s, ci:, :].astype(F32), 0.0)
            spot = (slice(s * ci, (s + 1) * ci), slice(b * bw, (b + 1) * bw))
            two[(1,) + spot] = (upre[spot] + 2.0 * u).astype(BF)
    g = nn(wt[K - 1, mine, :], two[0]).astype(BF)
    h = nn(w[K - 1], two[1]).astype(BF)
    gh2[0] = g
    gh2[1] = h
    sent = nn(h, op[:, own:]).astype(BF)
    t2 = two[0, mine, :]
    co = w.shape[2]
    wg2 = nt(t2, full[1])
    wg3 = 2.0 * nt(t2, full[3]) - wg[1]
    low[0:ci, 0:co] = wg[0]
    low[0:ci, co:] = wg[1]
    low[ci:, 0:co] = wg2
    low[ci:, co:] = wg3
    packed = low[...].astype(BF)
    gf = g.astype(F32)
    for o in range(n):
        blk = jnp.zeros((ci, bw), F32)
        for b in range(nb):
            blk = jnp.where(marks[o] == b, gf[:, b * bw : (b + 1) * bw], blk)
        x3[o, 0:ci, :] = blk.astype(BF)
        x3[o, ci : 2 * ci, :] = sent[:, o * bw : (o + 1) * bw]
        x3[o, 2 * ci :, :] = packed


def local_kernel(op, full, two, gh2, wt, w, outl, fgl):
    ci, own = outl.shape
    me = lax.axis_index("ch")
    mine = pl.ds(pl.multiple_of(me * ci, ci), ci)
    local = op[:, :own]
    out = nn(wt[0, mine, :], full[0]) + nn(wt[1, mine, :], full[2]) - nn(wt[3, mine, :], full[2])
    outl[...] = out + nn(wt[2, mine, :], two[0]) + 2.0 * nt(gh2[0], local)
    fg = nn(w[0], full[1]) + nn(w[1], full[3]) - nn(w[3], full[3])
    fgl[...] = fg + nn(w[2], two[1]) + 2.0 * nn(gh2[1], local)


def last_kernel(y3, marks_ref, op, outl, fgl, out, fg, wgrad, gh):
    n, ci, bw = marks_ref.shape
    own = outl.shape[1]
    nb = own // bw
    co = wgrad.shape[2]
    for o in range(n):
        gh[:, o * bw : (o + 1) * bw] = y3[o, 0:ci, :]
    out[...] = (outl[...] + 2.0 * nt(gh[...], op[:, own:])).astype(BF)
    for b in range(nb):
        u = jnp.zeros((ci, bw), F32)
        for o in range(n):
            u = u + jnp.where(marks_ref[o].astype(F32) == b, y3[o, ci : 2 * ci, :].astype(F32), 0.0)
        spot = slice(b * bw, (b + 1) * bw)
        fg[:, spot] = (fgl[:, spot] + 2.0 * u).astype(BF)
    wsum = y3[0, 2 * ci :, :].astype(F32)
    for o in range(1, n):
        wsum = wsum + y3[o, 2 * ci :, :].astype(F32)
    wgrad[0] = wsum[0:ci, 0:co]
    wgrad[1] = wsum[0:ci, co:]
    wgrad[2] = wsum[ci:, 0:co]
    wgrad[3] = wsum[ci:, co:]


def body(features, tiles, tile_cols, needs, weights, cotangent):
    ci, own = features.shape
    nb, tpr, bw, _ = tiles.shape
    co = weights.shape[2]
    n = lax.axis_size("rows")
    q = lax.axis_size("ch")
    total = ci * q
    cells = nb + n
    wide = cells * bw
    struct = jax.ShapeDtypeStruct
    smem = pl.BlockSpec(memory_space=SMEM)
    vmem = pl.BlockSpec(memory_space=VMEM)
    hbm = pl.BlockSpec(memory_space=pltpu.MemorySpace.HBM)
    limit = (16 << 20) + 4 * own * wide * 2
    params = pltpu.CompilerParams(vmem_limit_bytes=limit)
    packed = pltpu.CompilerParams(vmem_limit_bytes=62 << 20)

    needs = needs.reshape(1, n)
    x1, pack = pl.pallas_call(
        push_kernel,
        out_shape=(struct((n, (nb + 2) * ci, bw), BF), struct((3 * ci, own), BF)),
        in_specs=[hbm] * 6,
        out_specs=(vmem, vmem),
        scratch_shapes=[
            pltpu.SMEM((nb, tpr), jnp.int32),
            pltpu.SMEM((1, n), jnp.int32),
            pltpu.SMEM((nb * tpr,), jnp.int32),
            pltpu.SMEM((nb * tpr,), jnp.int32),
            pltpu.VMEM((ci, own), BF),
            pltpu.VMEM((ci, own), BF),
            pltpu.VMEM((K, ci, co), BF),
            pltpu.VMEM((nb * tpr, bw, bw), BF),
            pltpu.VMEM((n, ci, bw), F32),
            pltpu.SemaphoreType.DMA((5 + nb,)),
        ],
        compiler_params=packed,
        name="push",
    )(tile_cols, needs, features, cotangent, weights, tiles)
    y1 = lax.all_to_all(x1, "rows", 0, 0)

    op, lf, ltc = pl.pallas_call(
        combine_kernel,
        out_shape=(struct((own, wide), BF), struct((ci, own), F32), struct((ci, own), F32)),
        in_specs=[smem, vmem, vmem, hbm],
        out_specs=(vmem,) * 3,
        scratch_shapes=[
            pltpu.VMEM((bw, wide), F32),
            pltpu.VMEM((nb, tpr, bw, bw), BF),
            pltpu.SemaphoreType.DMA((nb,)),
        ],
        compiler_params=pltpu.CompilerParams(vmem_limit_bytes=51 << 20),
        cost_estimate=pl.CostEstimate(flops=4 * ci * own * own, bytes_accessed=8 << 20, transcendentals=0),
        name="combine",
    )(tile_cols, features, cotangent, tiles)

    def around(value):
        moved = [value]
        for s in range(1, q):
            moved.append(lax.ppermute(value, "ch", [(i, (i + s) % q) for i in range(q)]))
        return moved

    packs = around(pack)
    y1, *packs = lax.optimization_barrier((y1, *packs))

    x2, tu, marks = pl.pallas_call(
        first_kernel,
        out_shape=(struct((n * q, 2 * ci, bw), BF), struct((2 * ci, own), BF), struct((n, ci, bw), BF)),
        in_specs=[smem, vmem, vmem, vmem, vmem],
        out_specs=(vmem,) * 3,
        scratch_shapes=[pltpu.VMEM((ci, n * bw), BF)],
        compiler_params=params,
        name="first",
    )(needs, y1, op, lf, ltc)
    y2 = lax.all_to_all(x2, ("rows", "ch"), 0, 0)
    tus = around(tu)

    tpre, upre, full, wt, wg = pl.pallas_call(
        lambda *refs: gather_kernel(q, refs),
        out_shape=(
            struct((total, own), F32),
            struct((total, own), F32),
            struct((4, total, own), BF),
            struct((K, co, total), BF),
            struct((2, ci, co), F32),
        ),
        in_specs=[vmem] * (2 * q + 1),
        out_specs=(vmem,) * 5,
        scratch_shapes=[pltpu.VMEM((total, K * co), F32)],
        compiler_params=params,
        cost_estimate=pl.CostEstimate(flops=4 * total * own * own, bytes_accessed=4 << 20, transcendentals=0),
        name="gather",
    )(*packs, *tus, op)

    x3, two, gh2 = pl.pallas_call(
        functools.partial(second_kernel, q),
        out_shape=(struct((n, 4 * ci, bw), BF), struct((2, total, own), BF), struct((2, ci, own), BF)),
        in_specs=[vmem] * 9,
        out_specs=(vmem,) * 3,
        scratch_shapes=[pltpu.VMEM((total, n * bw), BF), pltpu.VMEM((2 * ci, bw), F32)],
        compiler_params=params,
        name="second",
    )(y2, marks, op, tpre, upre, full, wt, wg, weights)
    y3 = lax.all_to_all(x3, "rows", 0, 0)

    outl, fgl = pl.pallas_call(
        local_kernel,
        out_shape=(struct((ci, own), F32), struct((ci, own), F32)),
        in_specs=[vmem] * 6,
        out_specs=(vmem,) * 2,
        compiler_params=params,
        cost_estimate=pl.CostEstimate(flops=8 * total * ci * own, bytes_accessed=4 << 20, transcendentals=0),
        name="local",
    )(op, full, two, gh2, wt, weights)

    output, feature_grad, weight_grad = pl.pallas_call(
        last_kernel,
        out_shape=(struct((ci, own), BF), struct((ci, own), BF), struct((K, ci, co), F32)),
        in_specs=[vmem] * 5,
        out_specs=(vmem,) * 3,
        scratch_shapes=[pltpu.VMEM((ci, n * bw), BF)],
        compiler_params=params,
        name="last",
    )(y3, marks, op, outl, fgl)
    return output, feature_grad, weight_grad


def solution(mesh):
    placed = (
        P("ch", "rows"),
        P("rows", None, None, None),
        P("rows", None),
        P("rows", None, None),
        P(None, "ch", None),
        P("ch", "rows"),
    )
    return jax.shard_map(
        body,
        mesh=mesh,
        in_specs=placed,
        out_specs=(P("ch", "rows"), P("ch", "rows"), P(None, "ch", None)),
        check_vma=False,
    )
```

```python
import functools

import jax
import jax.numpy as jnp
from jax import lax
from jax.experimental import pallas as pl
from jax.experimental.pallas import tpu as pltpu
from jax.sharding import PartitionSpec as P

K = 4
BF = jnp.bfloat16
F32 = jnp.float32
SMEM = pltpu.MemorySpace.SMEM
VMEM = pltpu.MemorySpace.VMEM


def nn(a, b):
    return lax.dot_general(a, b, (((1,), (0,)), ((), ())), preferred_element_type=F32)


def nt(a, b):
    return lax.dot_general(a, b, (((1,), (1,)), ((), ())), preferred_element_type=F32)


def lanes(index, width):
    return pl.ds(pl.multiple_of(index * width, width), width)


def turn(n):
    return 5 * n // 8


def member(device, n):
    return (device - turn(n)) % n


def row_exchange(value, n):
    order = [(i + turn(n)) % n for i in range(n)]
    return lax.all_to_all(value, "rows", 0, 0, axis_index_groups=[order])


def push_kernel(cols_h, needs_h, f_h, c_h, tiles, x1, cols, needs, cells, where, f, c, buf, acc, sems):
    nb, tpr = cols.shape
    n, ci, bw = acc.shape
    small = [(cols_h, cols), (needs_h, needs), (f_h, f), (c_h, c)]
    copies = [pltpu.make_async_copy(src, dst, sems.at[i]) for i, (src, dst) in enumerate(small)]
    for r in range(nb):
        copies.append(pltpu.make_async_copy(tiles.at[r], buf.at[pl.ds(r * tpr, tpr)], sems.at[len(small) + r]))
    for copy in copies:
        copy.start()
    for o in range(n):
        acc[o] = jnp.zeros((ci, bw), F32)
    copies[0].wait()
    count = jnp.int32(0)
    for r in range(nb):
        for t in range(1, tpr):
            v = cols[r, t]
            cells[count] = v - nb
            where[count] = r * tpr + t
            count = count + (v >= nb).astype(jnp.int32)
    for copy in copies[1:4]:
        copy.wait()
    for o in range(n):
        for b in range(nb):
            x1[member(o, n), b * ci : (b + 1) * ci, :] = f[:, b * bw : (b + 1) * bw]
        x1[member(o, n), (nb + 1) * ci :, :] = jnp.full((8, bw), needs[0, o].astype(F32)).astype(BF)
    for copy in copies[4:]:
        copy.wait()

    def products(step, carry):
        for j in range(n):
            i = jnp.minimum(step * n + j, nb * tpr - 1)
            live = i < count
            o = jnp.where(live, cells[i], 0)
            at = jnp.where(live, where[i], 0)
            part = nn(c[:, lanes(at // tpr, bw)], buf[at])
            acc[o] += jnp.where(live, part, 0.0)
        return carry

    lax.fori_loop(0, (count + n - 1) // n, products, 0)
    for o in range(n):
        x1[member(o, n), nb * ci : (nb + 1) * ci, :] = acc[o].astype(BF)


def combine_kernel(cols, f, c, tiles, op, lf, ltc, total, buf, sems):
    nb, tpr = cols.shape
    bw = tiles.shape[2]
    own = f.shape[1]
    copies = [pltpu.make_async_copy(tiles.at[r], buf.at[r], sems.at[r]) for r in range(nb)]
    for copy in copies:
        copy.start()
    for r in range(nb):
        rows = slice(r * bw, (r + 1) * bw)
        total[...] = jnp.zeros_like(total)
        copies[r].wait()
        for t in range(tpr):
            at = lanes(cols[r, t], bw)
            total[:, at] += buf[r, t].astype(F32)
        op[rows, :] = total[...].astype(BF)
    local = op[:, :own]
    lf[...] = nt(f[...], local)
    ltc[...] = nn(c[...], local)


def first_kernel(needs, y1, op, lf, ltc, f, c, w, x2, tu, marks_ref, gh):
    n, rows, bw = y1.shape
    ci, own = lf.shape
    nb = own // bw
    q = x2.shape[0] // n
    for o in range(n):
        at = jnp.maximum(needs[0, o], 0) * ci
        gh[:, o * bw : (o + 1) * bw] = y1[member(o, n), pl.ds(pl.multiple_of(at, ci), ci), :]
    t1 = (lf[...] + nt(gh[...], op[:, own:])).astype(BF)
    marks = []
    for o in range(n):
        mark = y1[member(o, n), (nb + 1) * ci :, :].astype(F32)
        marks.append(jnp.concatenate([mark] * (ci // 8), axis=0))
        marks_ref[o] = marks[o].astype(BF)
    u1 = []
    for b in range(nb):
        u = ltc[:, b * bw : (b + 1) * bw]
        for o in range(n):
            u = u + jnp.where(marks[o] == b, y1[member(o, n), nb * ci : (nb + 1) * ci, :].astype(F32), 0.0)
        u1.append(u.astype(BF))
    for b in range(nb):
        tu[ci : 2 * ci, b * bw : (b + 1) * bw] = u1[b]
    sent = nn(tu[ci : 2 * ci], op[:, own:]).astype(BF)
    tu[0:ci] = t1
    tu[2 * ci : 3 * ci] = f[...]
    tu[3 * ci : 4 * ci] = c[...]
    co = w.shape[2]
    for k in range(K):
        tu[4 * ci :, k * co : (k + 1) * co] = w[k]
    tf = t1.astype(F32)
    for o in range(n):
        blk = jnp.zeros((ci, bw), F32)
        for b in range(nb):
            blk = jnp.where(marks[o] == b, tf[:, b * bw : (b + 1) * bw], blk)
        blk = blk.astype(BF)
        for s in range(q):
            x2[o * q + s, 0:ci, :] = blk
            x2[o * q + s, ci:, :] = sent[:, o * bw : (o + 1) * bw]


def gather_kernel(q, refs):
    tus, op, tpre, upre, full, wt, wg, wbuf = refs
    own = tpre.shape[1]
    total = tpre.shape[0]
    ci = total // q
    co = wt.shape[1]
    me = lax.axis_index("ch")
    for s in range(q):
        spot = slice(s * ci, (s + 1) * ci)
        full[0, spot, :] = tus[s][2 * ci : 3 * ci, :]
        full[1, spot, :] = tus[s][3 * ci : 4 * ci, :]
        full[2, spot, :] = tus[s][0:ci, :]
        full[3, spot, :] = tus[s][ci : 2 * ci, :]
        wbuf[spot, :] = tus[s][4 * ci :, : K * co].astype(F32)
    for k in range(K):
        turned = wbuf[:, k * co : (k + 1) * co].T
        wt[k] = turned.astype(BF)
    local = op[:, :own]
    tpre[...] = 2.0 * nt(full[2], local) - full[0].astype(F32)
    upre[...] = 2.0 * nn(full[3], local) - full[1].astype(F32)
    wg[0] = nt(tus[me, 2 * ci : 3 * ci, :], full[1])
    wg[1] = nt(tus[me, 0:ci, :], full[1])


def second_kernel(q, y2, marks_ref, op, tpre, upre, full, wt, wg, w, x3, two, gh2, gh, low):
    n, ci, bw = marks_ref.shape
    total, own = tpre.shape
    nb = own // bw
    me = lax.axis_index("ch")
    mine = pl.ds(pl.multiple_of(me * ci, ci), ci)
    for o in range(n):
        for s in range(q):
            gh[s * ci : (s + 1) * ci, o * bw : (o + 1) * bw] = y2[o * q + s, 0:ci, :]
    two[0] = (tpre[...] + 2.0 * nt(gh[...], op[:, own:])).astype(BF)
    marks = [marks_ref[o].astype(F32) for o in range(n)]
    for s in range(q):
        for b in range(nb):
            u = jnp.zeros((ci, bw), F32)
            for o in range(n):
                u = u + jnp.where(marks[o] == b, y2[o * q + s, ci:, :].astype(F32), 0.0)
            spot = (slice(s * ci, (s + 1) * ci), slice(b * bw, (b + 1) * bw))
            two[(1,) + spot] = (upre[spot] + 2.0 * u).astype(BF)
    g = nn(wt[K - 1, mine, :], two[0]).astype(BF)
    h = nn(w[K - 1], two[1]).astype(BF)
    gh2[0] = g
    gh2[1] = h
    sent = nn(h, op[:, own:]).astype(BF)
    t2 = two[0, mine, :]
    co = w.shape[2]
    wg2 = nt(t2, full[1])
    wg3 = 2.0 * nt(t2, full[3]) - wg[1]
    low[0:ci, 0:co] = wg[0]
    low[0:ci, co:] = wg[1]
    low[ci:, 0:co] = wg2
    low[ci:, co:] = wg3
    packed = low[...].astype(BF)
    gf = g.astype(F32)
    for o in range(n):
        blk = jnp.zeros((ci, bw), F32)
        for b in range(nb):
            blk = jnp.where(marks[o] == b, gf[:, b * bw : (b + 1) * bw], blk)
        x3[member(o, n), 0:ci, :] = blk.astype(BF)
        x3[member(o, n), ci : 2 * ci, :] = sent[:, o * bw : (o + 1) * bw]
        x3[member(o, n), 2 * ci :, :] = packed


def local_kernel(op, full, two, gh2, wt, w, outl, fgl):
    ci, own = outl.shape
    me = lax.axis_index("ch")
    mine = pl.ds(pl.multiple_of(me * ci, ci), ci)
    local = op[:, :own]
    out = nn(wt[0, mine, :], full[0]) + nn(wt[1, mine, :], full[2]) - nn(wt[3, mine, :], full[2])
    outl[...] = out + nn(wt[2, mine, :], two[0]) + 2.0 * nt(gh2[0], local)
    fg = nn(w[0], full[1]) + nn(w[1], full[3]) - nn(w[3], full[3])
    fgl[...] = fg + nn(w[2], two[1]) + 2.0 * nn(gh2[1], local)


def last_kernel(y3, marks_ref, op, outl, fgl, out, fg, wgrad, gh):
    n, ci, bw = marks_ref.shape
    own = outl.shape[1]
    nb = own // bw
    co = wgrad.shape[2]
    for o in range(n):
        gh[:, o * bw : (o + 1) * bw] = y3[member(o, n), 0:ci, :]
    out[...] = (outl[...] + 2.0 * nt(gh[...], op[:, own:])).astype(BF)
    for b in range(nb):
        u = jnp.zeros((ci, bw), F32)
        for o in range(n):
            u = u + jnp.where(marks_ref[o].astype(F32) == b, y3[member(o, n), ci : 2 * ci, :].astype(F32), 0.0)
        spot = slice(b * bw, (b + 1) * bw)
        fg[:, spot] = (fgl[:, spot] + 2.0 * u).astype(BF)
    wsum = y3[member(0, n), 2 * ci :, :].astype(F32)
    for o in range(1, n):
        wsum = wsum + y3[member(o, n), 2 * ci :, :].astype(F32)
    wgrad[0] = wsum[0:ci, 0:co]
    wgrad[1] = wsum[0:ci, co:]
    wgrad[2] = wsum[ci:, 0:co]
    wgrad[3] = wsum[ci:, co:]


def body(features, tiles, tile_cols, needs, weights, cotangent):
    ci, own = features.shape
    nb, tpr, bw, _ = tiles.shape
    co = weights.shape[2]
    n = lax.axis_size("rows")
    q = lax.axis_size("ch")
    total = ci * q
    cells = nb + n
    wide = cells * bw
    struct = jax.ShapeDtypeStruct
    smem = pl.BlockSpec(memory_space=SMEM)
    vmem = pl.BlockSpec(memory_space=VMEM)
    hbm = pl.BlockSpec(memory_space=pltpu.MemorySpace.HBM)
    limit = (16 << 20) + 4 * own * wide * 2
    params = pltpu.CompilerParams(vmem_limit_bytes=limit)
    packed = pltpu.CompilerParams(vmem_limit_bytes=62 << 20)

    needs = needs.reshape(1, n)
    x1 = pl.pallas_call(
        push_kernel,
        out_shape=struct((n, (nb + 1) * ci + 8, bw), BF),
        in_specs=[hbm] * 5,
        out_specs=vmem,
        scratch_shapes=[
            pltpu.SMEM((nb, tpr), jnp.int32),
            pltpu.SMEM((1, n), jnp.int32),
            pltpu.SMEM((nb * tpr,), jnp.int32),
            pltpu.SMEM((nb * tpr,), jnp.int32),
            pltpu.VMEM((ci, own), BF),
            pltpu.VMEM((ci, own), BF),
            pltpu.VMEM((nb * tpr, bw, bw), BF),
            pltpu.VMEM((n, ci, bw), F32),
            pltpu.SemaphoreType.DMA((4 + nb,)),
        ],
        compiler_params=packed,
        name="push",
    )(tile_cols, needs, features, cotangent, tiles)
    y1 = row_exchange(x1, n)

    op, lf, ltc = pl.pallas_call(
        combine_kernel,
        out_shape=(struct((own, wide), BF), struct((ci, own), F32), struct((ci, own), F32)),
        in_specs=[smem, vmem, vmem, hbm],
        out_specs=(vmem,) * 3,
        scratch_shapes=[
            pltpu.VMEM((bw, wide), F32),
            pltpu.VMEM((nb, tpr, bw, bw), BF),
            pltpu.SemaphoreType.DMA((nb,)),
        ],
        compiler_params=pltpu.CompilerParams(vmem_limit_bytes=51 << 20),
        cost_estimate=pl.CostEstimate(flops=4 * ci * own * own, bytes_accessed=8 << 20, transcendentals=0),
        name="combine",
    )(tile_cols, features, cotangent, tiles)

    x2, tu, marks = pl.pallas_call(
        first_kernel,
        out_shape=(struct((n * q, 2 * ci, bw), BF), struct((5 * ci, own), BF), struct((n, ci, bw), BF)),
        in_specs=[smem] + [vmem] * 7,
        out_specs=(vmem,) * 3,
        scratch_shapes=[pltpu.VMEM((ci, n * bw), BF)],
        compiler_params=params,
        name="first",
    )(needs, y1, op, lf, ltc, features, cotangent, weights)
    y2 = lax.all_to_all(x2, ("rows", "ch"), 0, 0)
    tus = lax.all_gather(tu, "ch", axis=0)

    tpre, upre, full, wt, wg = pl.pallas_call(
        lambda *refs: gather_kernel(q, refs),
        out_shape=(
            struct((total, own), F32),
            struct((total, own), F32),
            struct((4, total, own), BF),
            struct((K, co, total), BF),
            struct((2, ci, co), F32),
        ),
        in_specs=[vmem] * 2,
        out_specs=(vmem,) * 5,
        scratch_shapes=[pltpu.VMEM((total, K * co), F32)],
        compiler_params=params,
        cost_estimate=pl.CostEstimate(flops=4 * total * own * own, bytes_accessed=4 << 20, transcendentals=0),
        name="gather",
    )(tus, op)

    x3, two, gh2 = pl.pallas_call(
        functools.partial(second_kernel, q),
        out_shape=(struct((n, 4 * ci, bw), BF), struct((2, total, own), BF), struct((2, ci, own), BF)),
        in_specs=[vmem] * 9,
        out_specs=(vmem,) * 3,
        scratch_shapes=[pltpu.VMEM((total, n * bw), BF), pltpu.VMEM((2 * ci, bw), F32)],
        compiler_params=params,
        name="second",
    )(y2, marks, op, tpre, upre, full, wt, wg, weights)
    y3 = row_exchange(x3, n)

    outl, fgl = pl.pallas_call(
        local_kernel,
        out_shape=(struct((ci, own), F32), struct((ci, own), F32)),
        in_specs=[vmem] * 6,
        out_specs=(vmem,) * 2,
        compiler_params=params,
        cost_estimate=pl.CostEstimate(flops=8 * total * ci * own, bytes_accessed=4 << 20, transcendentals=0),
        name="local",
    )(op, full, two, gh2, wt, weights)

    output, feature_grad, weight_grad = pl.pallas_call(
        last_kernel,
        out_shape=(struct((ci, own), BF), struct((ci, own), BF), struct((K, ci, co), F32)),
        in_specs=[vmem] * 5,
        out_specs=(vmem,) * 3,
        scratch_shapes=[pltpu.VMEM((ci, n * bw), BF)],
        compiler_params=params,
        name="last",
    )(y3, marks, op, outl, fgl)
    return output, feature_grad, weight_grad


def solution(mesh):
    placed = (
        P("ch", "rows"),
        P("rows", None, None, None),
        P("rows", None),
        P("rows", None, None),
        P(None, "ch", None),
        P("ch", "rows"),
    )
    return jax.shard_map(
        body,
        mesh=mesh,
        in_specs=placed,
        out_specs=(P("ch", "rows"), P("ch", "rows"), P(None, "ch", None)),
        check_vma=False,
    )
```

```python
import functools

import jax
import jax.numpy as jnp
from jax import lax
from jax.experimental import pallas as pl
from jax.experimental.pallas import tpu as pltpu
from jax.sharding import PartitionSpec as P

K = 4
BF = jnp.bfloat16
F32 = jnp.float32
SMEM = pltpu.MemorySpace.SMEM
VMEM = pltpu.MemorySpace.VMEM


def nn(a, b):
    return lax.dot_general(a, b, (((1,), (0,)), ((), ())), preferred_element_type=F32)


def nt(a, b):
    return lax.dot_general(a, b, (((1,), (1,)), ((), ())), preferred_element_type=F32)


def lanes(index, width):
    return pl.ds(pl.multiple_of(index * width, width), width)


def turn(n):
    return 5 * n // 8


def member(device, n):
    return (device - turn(n)) % n


def row_exchange(value, n):
    order = [(i + turn(n)) % n for i in range(n)]
    return lax.all_to_all(value, "rows", 0, 0, axis_index_groups=[order])


def spread(device, pair, n, half):
    return (device * half + pair - turn(n) * half) % (n * half)


def spread_exchange(value, n, q):
    half = q // 2
    groups = []
    for parity in range(2):
        members = [row * q + 2 * pair + parity for row in range(n) for pair in range(half)]
        start = turn(n) * half
        groups.append(members[start:] + members[:start])
    return lax.all_to_all(value, ("rows", "ch"), 0, 0, axis_index_groups=groups)


def swap(value, q, bit):
    return lax.ppermute(value, "ch", [(i, i ^ bit) for i in range(q)])


def push_kernel(cols_h, needs_h, f_h, c_h, w_h, tiles, x1, pack, cols, needs, cells, where, f, c, w, buf, acc, sems):
    nb, tpr = cols.shape
    n, ci, bw = acc.shape
    small = [(cols_h, cols), (needs_h, needs), (f_h, f), (c_h, c), (w_h, w)]
    copies = [pltpu.make_async_copy(src, dst, sems.at[i]) for i, (src, dst) in enumerate(small)]
    for r in range(nb):
        copies.append(pltpu.make_async_copy(tiles.at[r], buf.at[pl.ds(r * tpr, tpr)], sems.at[len(small) + r]))
    for copy in copies:
        copy.start()
    for o in range(n):
        acc[o] = jnp.zeros((ci, bw), F32)
    copies[0].wait()
    count = jnp.int32(0)
    for r in range(nb):
        for t in range(1, tpr):
            v = cols[r, t]
            cells[count] = v - nb
            where[count] = r * tpr + t
            count = count + (v >= nb).astype(jnp.int32)
    for copy in copies[1:5]:
        copy.wait()
    for o in range(n):
        for b in range(nb):
            x1[member(o, n), b * ci : (b + 1) * ci, :] = f[:, b * bw : (b + 1) * bw]
        x1[member(o, n), (nb + 1) * ci :, :] = jnp.full((8, bw), needs[0, o].astype(F32)).astype(BF)
    pack[0:ci] = f[...]
    pack[ci : 2 * ci] = c[...]
    for k in range(K):
        width = w.shape[2]
        pack[2 * ci :, k * width : (k + 1) * width] = w[k]
    for copy in copies[5:]:
        copy.wait()

    def products(step, carry):
        for j in range(n):
            i = jnp.minimum(step * n + j, nb * tpr - 1)
            live = i < count
            o = jnp.where(live, cells[i], 0)
            at = jnp.where(live, where[i], 0)
            part = nn(c[:, lanes(at // tpr, bw)], buf[at])
            acc[o] += jnp.where(live, part, 0.0)
        return carry

    lax.fori_loop(0, (count + n - 1) // n, products, 0)
    for o in range(n):
        x1[member(o, n), nb * ci : (nb + 1) * ci, :] = acc[o].astype(BF)


def combine_kernel(cols, f, c, tiles, op, lf, ltc, total, buf, sems):
    nb, tpr = cols.shape
    bw = tiles.shape[2]
    own = f.shape[1]
    copies = [pltpu.make_async_copy(tiles.at[r], buf.at[r], sems.at[r]) for r in range(nb)]
    for copy in copies:
        copy.start()
    for r in range(nb):
        rows = slice(r * bw, (r + 1) * bw)
        total[...] = jnp.zeros_like(total)
        copies[r].wait()
        for t in range(tpr):
            at = lanes(cols[r, t], bw)
            total[:, at] += buf[r, t].astype(F32)
        op[rows, :] = total[...].astype(BF)
    local = op[:, :own]
    lf[...] = nt(f[...], local)
    ltc[...] = nn(c[...], local)


def first_kernel(needs, y1, op, lf, ltc, x2, tu, marks_ref, gh):
    n, rows, bw = y1.shape
    ci, own = lf.shape
    nb = own // bw
    half = x2.shape[0] // n
    for o in range(n):
        at = jnp.maximum(needs[0, o], 0) * ci
        gh[:, o * bw : (o + 1) * bw] = y1[member(o, n), pl.ds(pl.multiple_of(at, ci), ci), :]
    t1 = (lf[...] + nt(gh[...], op[:, own:])).astype(BF)
    marks = []
    for o in range(n):
        mark = y1[member(o, n), (nb + 1) * ci :, :].astype(F32)
        marks.append(jnp.concatenate([mark] * (ci // 8), axis=0))
        marks_ref[o] = marks[o].astype(BF)
    u1 = []
    for b in range(nb):
        u = ltc[:, b * bw : (b + 1) * bw]
        for o in range(n):
            u = u + jnp.where(marks[o] == b, y1[member(o, n), nb * ci : (nb + 1) * ci, :].astype(F32), 0.0)
        u1.append(u.astype(BF))
    for b in range(nb):
        tu[ci : 2 * ci, b * bw : (b + 1) * bw] = u1[b]
    sent = nn(tu[ci : 2 * ci], op[:, own:]).astype(BF)
    tu[0:ci] = t1
    tf = t1.astype(F32)
    for o in range(n):
        blk = jnp.zeros((ci, bw), F32)
        for b in range(nb):
            blk = jnp.where(marks[o] == b, tf[:, b * bw : (b + 1) * bw], blk)
        blk = blk.astype(BF)
        for s in range(half):
            x2[spread(o, s, n, half), 0:ci, :] = blk
            x2[spread(o, s, n, half), ci:, :] = sent[:, o * bw : (o + 1) * bw]


def gather_kernel(q, refs):
    packs = refs[:q]
    tus = refs[q : 2 * q]
    op, w, tpre, upre, full, wt, wg, outl, fgl, wbuf = refs[2 * q :]
    own = tpre.shape[1]
    total = tpre.shape[0]
    ci = total // q
    co = wt.shape[1]
    me = lax.axis_index("ch")
    for s in range(q):
        spot = pl.ds(pl.multiple_of((me ^ s) * ci, ci), ci)
        full[0, spot, :] = packs[s][0:ci, :]
        full[1, spot, :] = packs[s][ci : 2 * ci, :]
        full[2, spot, :] = tus[s][0:ci, :]
        full[3, spot, :] = tus[s][ci : 2 * ci, :]
        wbuf[spot, :] = packs[s][2 * ci :, : K * co].astype(F32)
    for k in range(K):
        turned = wbuf[:, k * co : (k + 1) * co].T
        wt[k] = turned.astype(BF)
    mine = pl.ds(pl.multiple_of(me * ci, ci), ci)
    outl[...] = nn(wt[0, mine, :], full[0]) + nn(wt[1, mine, :], full[2]) - nn(wt[3, mine, :], full[2])
    fgl[...] = nn(w[0], full[1]) + nn(w[1], full[3]) - nn(w[3], full[3])
    local = op[:, :own]
    tpre[...] = 2.0 * nt(full[2], local) - full[0].astype(F32)
    upre[...] = 2.0 * nn(full[3], local) - full[1].astype(F32)
    wg[0] = nt(packs[0][0:ci, :], full[1])
    wg[1] = nt(tus[0][0:ci, :], full[1])


def second_kernel(q, y2, z2, marks_ref, op, tpre, upre, full, wt, wg, w, x3, two, gh2, gh, low):
    n, ci, bw = marks_ref.shape
    total, own = tpre.shape
    nb = own // bw
    me = lax.axis_index("ch")
    mine = pl.ds(pl.multiple_of(me * ci, ci), ci)
    half = q // 2
    sources = []
    for s in range(half):
        own_at = 2 * s + me % 2
        sources.append((s, y2, pl.ds(pl.multiple_of(own_at * ci, ci), ci)))
        sources.append((s, z2, pl.ds(pl.multiple_of((own_at ^ 1) * ci, ci), ci)))
    for o in range(n):
        for s, came, spot in sources:
            gh[spot, o * bw : (o + 1) * bw] = came[spread(o, s, n, half), 0:ci, :]
    two[0] = (tpre[...] + 2.0 * nt(gh[...], op[:, own:])).astype(BF)
    marks = [marks_ref[o].astype(F32) for o in range(n)]
    for s, came, spot in sources:
        for b in range(nb):
            u = jnp.zeros((ci, bw), F32)
            for o in range(n):
                u = u + jnp.where(marks[o] == b, came[spread(o, s, n, half), ci:, :].astype(F32), 0.0)
            at = (spot, slice(b * bw, (b + 1) * bw))
            two[(1,) + at] = (upre[at] + 2.0 * u).astype(BF)
    g = nn(wt[K - 1, mine, :], two[0]).astype(BF)
    h = nn(w[K - 1], two[1]).astype(BF)
    gh2[0] = g
    gh2[1] = h
    sent = nn(h, op[:, own:]).astype(BF)
    t2 = two[0, mine, :]
    co = w.shape[2]
    wg2 = nt(t2, full[1])
    wg3 = 2.0 * nt(t2, full[3]) - wg[1]
    low[0:ci, 0:co] = wg[0]
    low[0:ci, co:] = wg[1]
    low[ci:, 0:co] = wg2
    low[ci:, co:] = wg3
    packed = low[...].astype(BF)
    gf = g.astype(F32)
    for o in range(n):
        blk = jnp.zeros((ci, bw), F32)
        for b in range(nb):
            blk = jnp.where(marks[o] == b, gf[:, b * bw : (b + 1) * bw], blk)
        x3[member(o, n), 0:ci, :] = blk.astype(BF)
        x3[member(o, n), ci : 2 * ci, :] = sent[:, o * bw : (o + 1) * bw]
        x3[member(o, n), 2 * ci :, :] = packed


def last_kernel(y3, marks_ref, op, outl, fgl, two, gh2, wt, w, out, fg, wgrad, gh):
    n, ci, bw = marks_ref.shape
    own = outl.shape[1]
    nb = own // bw
    co = wgrad.shape[2]
    me = lax.axis_index("ch")
    mine = pl.ds(pl.multiple_of(me * ci, ci), ci)
    gh[:, :own] = gh2[0]
    for o in range(n):
        gh[:, own + o * bw : own + (o + 1) * bw] = y3[member(o, n), 0:ci, :]
    out[...] = (outl[...] + nn(wt[2, mine, :], two[0]) + 2.0 * nt(gh[...], op[...])).astype(BF)
    back = nn(gh2[1], op[:, :own])
    base = fgl[...] + nn(w[2], two[1])
    for b in range(nb):
        spot = slice(b * bw, (b + 1) * bw)
        u = back[:, spot]
        for o in range(n):
            u = u + jnp.where(marks_ref[o].astype(F32) == b, y3[member(o, n), ci : 2 * ci, :].astype(F32), 0.0)
        fg[:, spot] = (base[:, spot] + 2.0 * u).astype(BF)
    wsum = y3[member(0, n), 2 * ci :, :].astype(F32)
    for o in range(1, n):
        wsum = wsum + y3[member(o, n), 2 * ci :, :].astype(F32)
    wgrad[0] = wsum[0:ci, 0:co]
    wgrad[1] = wsum[0:ci, co:]
    wgrad[2] = wsum[ci:, 0:co]
    wgrad[3] = wsum[ci:, co:]


def body(features, tiles, tile_cols, needs, weights, cotangent):
    ci, own = features.shape
    nb, tpr, bw, _ = tiles.shape
    co = weights.shape[2]
    n = lax.axis_size("rows")
    q = lax.axis_size("ch")
    total = ci * q
    cells = nb + n
    wide = cells * bw
    struct = jax.ShapeDtypeStruct
    smem = pl.BlockSpec(memory_space=SMEM)
    vmem = pl.BlockSpec(memory_space=VMEM)
    hbm = pl.BlockSpec(memory_space=pltpu.MemorySpace.HBM)
    limit = (16 << 20) + 4 * own * wide * 2
    params = pltpu.CompilerParams(vmem_limit_bytes=limit)
    packed = pltpu.CompilerParams(vmem_limit_bytes=62 << 20)

    needs = needs.reshape(1, n)
    x1, pack = pl.pallas_call(
        push_kernel,
        out_shape=(struct((n, (nb + 1) * ci + 8, bw), BF), struct((3 * ci, own), BF)),
        in_specs=[hbm] * 6,
        out_specs=(vmem, vmem),
        scratch_shapes=[
            pltpu.SMEM((nb, tpr), jnp.int32),
            pltpu.SMEM((1, n), jnp.int32),
            pltpu.SMEM((nb * tpr,), jnp.int32),
            pltpu.SMEM((nb * tpr,), jnp.int32),
            pltpu.VMEM((ci, own), BF),
            pltpu.VMEM((ci, own), BF),
            pltpu.VMEM((K, ci, co), BF),
            pltpu.VMEM((nb * tpr, bw, bw), BF),
            pltpu.VMEM((n, ci, bw), F32),
            pltpu.SemaphoreType.DMA((5 + nb,)),
        ],
        compiler_params=packed,
        name="push",
    )(tile_cols, needs, features, cotangent, weights, tiles)
    y1 = row_exchange(x1, n)

    op, lf, ltc = pl.pallas_call(
        combine_kernel,
        out_shape=(struct((own, wide), BF), struct((ci, own), F32), struct((ci, own), F32)),
        in_specs=[smem, vmem, vmem, hbm],
        out_specs=(vmem,) * 3,
        scratch_shapes=[
            pltpu.VMEM((bw, wide), F32),
            pltpu.VMEM((nb, tpr, bw, bw), BF),
            pltpu.SemaphoreType.DMA((nb,)),
        ],
        compiler_params=pltpu.CompilerParams(vmem_limit_bytes=51 << 20),
        cost_estimate=pl.CostEstimate(flops=4 * ci * own * own, bytes_accessed=8 << 20, transcendentals=0),
        name="combine",
    )(tile_cols, features, cotangent, tiles)

    packs = [pack, swap(pack, q, 1), swap(pack, q, 2), swap(pack, q, 3)]
    y1, *packs[1:] = lax.optimization_barrier((y1, *packs[1:]))

    x2, tu, marks = pl.pallas_call(
        first_kernel,
        out_shape=(struct((n * (q // 2), 2 * ci, bw), BF), struct((2 * ci, own), BF), struct((n, ci, bw), BF)),
        in_specs=[smem] + [vmem] * 4,
        out_specs=(vmem,) * 3,
        scratch_shapes=[pltpu.VMEM((ci, n * bw), BF)],
        compiler_params=params,
        name="first",
    )(needs, y1, op, lf, ltc)
    y2 = spread_exchange(x2, n, q)
    tus = [tu, swap(tu, q, 1), swap(tu, q, 2)]
    tus.append(swap(tu, q, 3))
    y2, *tus[1:] = lax.optimization_barrier((y2, *tus[1:]))
    z2 = swap(y2, q, 1)

    tpre, upre, full, wt, wg, outl, fgl = pl.pallas_call(
        lambda *refs: gather_kernel(q, refs),
        out_shape=(
            struct((total, own), F32),
            struct((total, own), F32),
            struct((4, total, own), BF),
            struct((K, co, total), BF),
            struct((2, ci, co), F32),
            struct((ci, own), F32),
            struct((ci, own), F32),
        ),
        in_specs=[vmem] * (2 * q + 2),
        out_specs=(vmem,) * 7,
        scratch_shapes=[pltpu.VMEM((total, K * co), F32)],
        compiler_params=params,
        cost_estimate=pl.CostEstimate(flops=4 * total * own * own, bytes_accessed=4 << 20, transcendentals=0),
        name="gather",
    )(*packs, *tus, op, weights)

    x3, two, gh2 = pl.pallas_call(
        functools.partial(second_kernel, q),
        out_shape=(struct((n, 4 * ci, bw), BF), struct((2, total, own), BF), struct((2, ci, own), BF)),
        in_specs=[vmem] * 10,
        out_specs=(vmem,) * 3,
        scratch_shapes=[pltpu.VMEM((total, n * bw), BF), pltpu.VMEM((2 * ci, bw), F32)],
        compiler_params=params,
        name="second",
    )(y2, z2, marks, op, tpre, upre, full, wt, wg, weights)
    y3 = row_exchange(x3, n)

    output, feature_grad, weight_grad = pl.pallas_call(
        last_kernel,
        out_shape=(struct((ci, own), BF), struct((ci, own), BF), struct((K, ci, co), F32)),
        in_specs=[vmem] * 9,
        out_specs=(vmem,) * 3,
        scratch_shapes=[pltpu.VMEM((ci, wide), BF)],
        compiler_params=params,
        name="last",
    )(y3, marks, op, outl, fgl, two, gh2, wt, weights)
    return output, feature_grad, weight_grad


def solution(mesh):
    placed = (
        P("ch", "rows"),
        P("rows", None, None, None),
        P("rows", None),
        P("rows", None, None),
        P(None, "ch", None),
        P("ch", "rows"),
    )
    return jax.shard_map(
        body,
        mesh=mesh,
        in_specs=placed,
        out_specs=(P("ch", "rows"), P("ch", "rows"), P(None, "ch", None)),
        check_vma=False,
    )
```

```python
import functools

import jax
import jax.numpy as jnp
from jax import lax
from jax.experimental import pallas as pl
from jax.experimental.pallas import tpu as pltpu
from jax.sharding import PartitionSpec as P

K = 4
BF = jnp.bfloat16
F32 = jnp.float32
SMEM = pltpu.MemorySpace.SMEM
VMEM = pltpu.MemorySpace.VMEM


def nn(a, b):
    return lax.dot_general(a, b, (((1,), (0,)), ((), ())), preferred_element_type=F32)


def nt(a, b):
    return lax.dot_general(a, b, (((1,), (1,)), ((), ())), preferred_element_type=F32)


def lanes(index, width):
    return pl.ds(pl.multiple_of(index * width, width), width)


def turn(n):
    return 5 * n // 8


def member(device, n):
    return (device - turn(n)) % n


def row_exchange(value, n):
    order = [(i + turn(n)) % n for i in range(n)]
    return lax.all_to_all(value, "rows", 0, 0, axis_index_groups=[order])


def spread(device, pair, n, half):
    return (device * half + pair - turn(n) * half - 1) % (n * half)


def spread_exchange(value, n, q):
    half = q // 2
    groups = []
    for parity in range(2):
        members = [row * q + 2 * pair + parity for row in range(n) for pair in range(half)]
        start = turn(n) * half + 1
        groups.append(members[start:] + members[:start])
    return lax.all_to_all(value, ("rows", "ch"), 0, 0, axis_index_groups=groups)


def swap(value, q, bit):
    return lax.ppermute(value, "ch", [(i, i ^ bit) for i in range(q)])


def push_kernel(cols_h, needs_h, f_h, c_h, w_h, tiles, x1, pack, cols, needs, cells, where, f, c, w, buf, acc, sems):
    nb, tpr = cols.shape
    n, ci, bw = acc.shape
    small = [(cols_h, cols), (needs_h, needs), (f_h, f), (c_h, c), (w_h, w)]
    copies = [pltpu.make_async_copy(src, dst, sems.at[i]) for i, (src, dst) in enumerate(small)]
    for r in range(nb):
        copies.append(pltpu.make_async_copy(tiles.at[r], buf.at[pl.ds(r * tpr, tpr)], sems.at[len(small) + r]))
    for copy in copies:
        copy.start()
    for o in range(n):
        acc[o] = jnp.zeros((ci, bw), F32)
    copies[0].wait()
    count = jnp.int32(0)
    for r in range(nb):
        for t in range(1, tpr):
            v = cols[r, t]
            cells[count] = v - nb
            where[count] = r * tpr + t
            count = count + (v >= nb).astype(jnp.int32)
    for copy in copies[1:5]:
        copy.wait()
    for o in range(n):
        for b in range(nb):
            x1[member(o, n), b * ci : (b + 1) * ci, :] = f[:, b * bw : (b + 1) * bw]
        x1[member(o, n), (nb + 1) * ci :, :] = jnp.full((8, bw), needs[0, o].astype(F32)).astype(BF)
    pack[0:ci] = f[...]
    pack[ci : 2 * ci] = c[...]
    for k in range(K):
        width = w.shape[2]
        pack[2 * ci :, k * width : (k + 1) * width] = w[k]
    for copy in copies[5:]:
        copy.wait()

    def products(step, carry):
        for j in range(n):
            i = jnp.minimum(step * n + j, nb * tpr - 1)
            live = i < count
            o = jnp.where(live, cells[i], 0)
            at = jnp.where(live, where[i], 0)
            part = nn(c[:, lanes(at // tpr, bw)], buf[at])
            acc[o] += jnp.where(live, part, 0.0)
        return carry

    lax.fori_loop(0, (count + n - 1) // n, products, 0)
    for o in range(n):
        x1[member(o, n), nb * ci : (nb + 1) * ci, :] = acc[o].astype(BF)


def combine_kernel(cols, f, c, tiles, op, lf, ltc, total, buf, sems):
    nb, tpr = cols.shape
    bw = tiles.shape[2]
    own = f.shape[1]
    copies = [pltpu.make_async_copy(tiles.at[r], buf.at[r], sems.at[r]) for r in range(nb)]
    for copy in copies:
        copy.start()
    for r in range(nb):
        rows = slice(r * bw, (r + 1) * bw)
        total[...] = jnp.zeros_like(total)
        copies[r].wait()
        for t in range(tpr):
            at = lanes(cols[r, t], bw)
            total[:, at] += buf[r, t].astype(F32)
        op[rows, :] = total[...].astype(BF)
    local = op[:, :own]
    lf[...] = nt(f[...], local)
    ltc[...] = nn(c[...], local)


def first_kernel(needs, y1, op, lf, ltc, x2, tu, marks_ref, gh):
    n, rows, bw = y1.shape
    ci, own = lf.shape
    nb = own // bw
    half = x2.shape[0] // n
    for o in range(n):
        at = jnp.maximum(needs[0, o], 0) * ci
        gh[:, o * bw : (o + 1) * bw] = y1[member(o, n), pl.ds(pl.multiple_of(at, ci), ci), :]
    t1 = (lf[...] + nt(gh[...], op[:, own:])).astype(BF)
    marks = []
    for o in range(n):
        mark = y1[member(o, n), (nb + 1) * ci :, :].astype(F32)
        marks.append(jnp.concatenate([mark] * (ci // 8), axis=0))
        marks_ref[o] = marks[o].astype(BF)
    u1 = []
    for b in range(nb):
        u = ltc[:, b * bw : (b + 1) * bw]
        for o in range(n):
            u = u + jnp.where(marks[o] == b, y1[member(o, n), nb * ci : (nb + 1) * ci, :].astype(F32), 0.0)
        u1.append(u.astype(BF))
    for b in range(nb):
        tu[ci : 2 * ci, b * bw : (b + 1) * bw] = u1[b]
    sent = nn(tu[ci : 2 * ci], op[:, own:]).astype(BF)
    tu[0:ci] = t1
    tf = t1.astype(F32)
    for o in range(n):
        blk = jnp.zeros((ci, bw), F32)
        for b in range(nb):
            blk = jnp.where(marks[o] == b, tf[:, b * bw : (b + 1) * bw], blk)
        blk = blk.astype(BF)
        for s in range(half):
            x2[spread(o, s, n, half), 0:ci, :] = blk
            x2[spread(o, s, n, half), ci:, :] = sent[:, o * bw : (o + 1) * bw]


def gather_kernel(q, refs):
    packs = refs[:q]
    tus = refs[q : 2 * q]
    op, w, tpre, upre, full, wt, wg, outl, fgl, wbuf = refs[2 * q :]
    own = tpre.shape[1]
    total = tpre.shape[0]
    ci = total // q
    co = wt.shape[1]
    me = lax.axis_index("ch")
    for s in range(q):
        spot = pl.ds(pl.multiple_of((me ^ s) * ci, ci), ci)
        full[0, spot, :] = packs[s][0:ci, :]
        full[1, spot, :] = packs[s][ci : 2 * ci, :]
        full[2, spot, :] = tus[s][0:ci, :]
        full[3, spot, :] = tus[s][ci : 2 * ci, :]
        wbuf[spot, :] = packs[s][2 * ci :, : K * co].astype(F32)
    for k in range(K):
        turned = wbuf[:, k * co : (k + 1) * co].T
        wt[k] = turned.astype(BF)
    mine = pl.ds(pl.multiple_of(me * ci, ci), ci)
    outl[...] = nn(wt[0, mine, :], full[0]) + nn(wt[1, mine, :], full[2]) - nn(wt[3, mine, :], full[2])
    fgl[...] = nn(w[0], full[1]) + nn(w[1], full[3]) - nn(w[3], full[3])
    local = op[:, :own]
    tpre[...] = 2.0 * nt(full[2], local) - full[0].astype(F32)
    upre[...] = 2.0 * nn(full[3], local) - full[1].astype(F32)
    wg[0] = nt(packs[0][0:ci, :], full[1])
    wg[1] = nt(tus[0][0:ci, :], full[1])


def second_kernel(q, y2, z2, marks_ref, op, tpre, upre, full, wt, wg, w, x3, two, gh2, gh, low):
    n, ci, bw = marks_ref.shape
    total, own = tpre.shape
    nb = own // bw
    me = lax.axis_index("ch")
    mine = pl.ds(pl.multiple_of(me * ci, ci), ci)
    half = q // 2
    sources = []
    for s in range(half):
        own_at = 2 * s + me % 2
        sources.append((s, y2, pl.ds(pl.multiple_of(own_at * ci, ci), ci)))
        sources.append((s, z2, pl.ds(pl.multiple_of((own_at ^ 1) * ci, ci), ci)))
    for o in range(n):
        for s, came, spot in sources:
            gh[spot, o * bw : (o + 1) * bw] = came[spread(o, s, n, half), 0:ci, :]
    two[0] = (tpre[...] + 2.0 * nt(gh[...], op[:, own:])).astype(BF)
    marks = [marks_ref[o].astype(F32) for o in range(n)]
    for s, came, spot in sources:
        for b in range(nb):
            u = jnp.zeros((ci, bw), F32)
            for o in range(n):
                u = u + jnp.where(marks[o] == b, came[spread(o, s, n, half), ci:, :].astype(F32), 0.0)
            at = (spot, slice(b * bw, (b + 1) * bw))
            two[(1,) + at] = (upre[at] + 2.0 * u).astype(BF)
    g = nn(wt[K - 1, mine, :], two[0]).astype(BF)
    h = nn(w[K - 1], two[1]).astype(BF)
    gh2[0] = g
    gh2[1] = h
    sent = nn(h, op[:, own:]).astype(BF)
    t2 = two[0, mine, :]
    co = w.shape[2]
    wg2 = nt(t2, full[1])
    wg3 = 2.0 * nt(t2, full[3]) - wg[1]
    low[0:ci, 0:co] = wg[0]
    low[0:ci, co:] = wg[1]
    low[ci:, 0:co] = wg2
    low[ci:, co:] = wg3
    packed = low[...].astype(BF)
    gf = g.astype(F32)
    for o in range(n):
        blk = jnp.zeros((ci, bw), F32)
        for b in range(nb):
            blk = jnp.where(marks[o] == b, gf[:, b * bw : (b + 1) * bw], blk)
        x3[member(o, n), 0:ci, :] = blk.astype(BF)
        x3[member(o, n), ci : 2 * ci, :] = sent[:, o * bw : (o + 1) * bw]
        x3[member(o, n), 2 * ci :, :] = packed


def last_kernel(y3, marks_ref, op, outl, fgl, two, gh2, wt, w, out, fg, wgrad, gh):
    n, ci, bw = marks_ref.shape
    own = outl.shape[1]
    nb = own // bw
    co = wgrad.shape[2]
    me = lax.axis_index("ch")
    mine = pl.ds(pl.multiple_of(me * ci, ci), ci)
    gh[:, :own] = gh2[0]
    for o in range(n):
        gh[:, own + o * bw : own + (o + 1) * bw] = y3[member(o, n), 0:ci, :]
    out[...] = (outl[...] + nn(wt[2, mine, :], two[0]) + 2.0 * nt(gh[...], op[...])).astype(BF)
    back = nn(gh2[1], op[:, :own])
    base = fgl[...] + nn(w[2], two[1])
    for b in range(nb):
        spot = slice(b * bw, (b + 1) * bw)
        u = back[:, spot]
        for o in range(n):
            u = u + jnp.where(marks_ref[o].astype(F32) == b, y3[member(o, n), ci : 2 * ci, :].astype(F32), 0.0)
        fg[:, spot] = (base[:, spot] + 2.0 * u).astype(BF)
    wsum = y3[member(0, n), 2 * ci :, :].astype(F32)
    for o in range(1, n):
        wsum = wsum + y3[member(o, n), 2 * ci :, :].astype(F32)
    wgrad[0] = wsum[0:ci, 0:co]
    wgrad[1] = wsum[0:ci, co:]
    wgrad[2] = wsum[ci:, 0:co]
    wgrad[3] = wsum[ci:, co:]


def body(features, tiles, tile_cols, needs, weights, cotangent):
    ci, own = features.shape
    nb, tpr, bw, _ = tiles.shape
    co = weights.shape[2]
    n = lax.axis_size("rows")
    q = lax.axis_size("ch")
    total = ci * q
    cells = nb + n
    wide = cells * bw
    struct = jax.ShapeDtypeStruct
    smem = pl.BlockSpec(memory_space=SMEM)
    vmem = pl.BlockSpec(memory_space=VMEM)
    hbm = pl.BlockSpec(memory_space=pltpu.MemorySpace.HBM)
    limit = (16 << 20) + 4 * own * wide * 2
    params = pltpu.CompilerParams(vmem_limit_bytes=limit)
    packed = pltpu.CompilerParams(vmem_limit_bytes=62 << 20)

    needs = needs.reshape(1, n)
    x1, pack = pl.pallas_call(
        push_kernel,
        out_shape=(struct((n, (nb + 1) * ci + 8, bw), BF), struct((3 * ci, own), BF)),
        in_specs=[hbm] * 6,
        out_specs=(vmem, vmem),
        scratch_shapes=[
            pltpu.SMEM((nb, tpr), jnp.int32),
            pltpu.SMEM((1, n), jnp.int32),
            pltpu.SMEM((nb * tpr,), jnp.int32),
            pltpu.SMEM((nb * tpr,), jnp.int32),
            pltpu.VMEM((ci, own), BF),
            pltpu.VMEM((ci, own), BF),
            pltpu.VMEM((K, ci, co), BF),
            pltpu.VMEM((nb * tpr, bw, bw), BF),
            pltpu.VMEM((n, ci, bw), F32),
            pltpu.SemaphoreType.DMA((5 + nb,)),
        ],
        compiler_params=packed,
        name="push",
    )(tile_cols, needs, features, cotangent, weights, tiles)
    y1 = row_exchange(x1, n)

    op, lf, ltc = pl.pallas_call(
        combine_kernel,
        out_shape=(struct((own, wide), BF), struct((ci, own), F32), struct((ci, own), F32)),
        in_specs=[smem, vmem, vmem, hbm],
        out_specs=(vmem,) * 3,
        scratch_shapes=[
            pltpu.VMEM((bw, wide), F32),
            pltpu.VMEM((nb, tpr, bw, bw), BF),
            pltpu.SemaphoreType.DMA((nb,)),
        ],
        compiler_params=pltpu.CompilerParams(vmem_limit_bytes=51 << 20),
        cost_estimate=pl.CostEstimate(flops=4 * ci * own * own, bytes_accessed=8 << 20, transcendentals=0),
        name="combine",
    )(tile_cols, features, cotangent, tiles)

    packs = [pack, swap(pack, q, 1), swap(pack, q, 2), swap(pack, q, 3)]
    y1, *packs[1:] = lax.optimization_barrier((y1, *packs[1:]))

    x2, tu, marks = pl.pallas_call(
        first_kernel,
        out_shape=(struct((n * (q // 2), 2 * ci, bw), BF), struct((2 * ci, own), BF), struct((n, ci, bw), BF)),
        in_specs=[smem] + [vmem] * 4,
        out_specs=(vmem,) * 3,
        scratch_shapes=[pltpu.VMEM((ci, n * bw), BF)],
        compiler_params=params,
        name="first",
    )(needs, y1, op, lf, ltc)
    y2 = spread_exchange(x2, n, q)
    tus = [tu, swap(tu, q, 1), swap(tu, q, 2)]
    tus.append(swap(tu, q, 3))
    y2, *tus[1:] = lax.optimization_barrier((y2, *tus[1:]))
    z2 = swap(y2, q, 1)

    tpre, upre, full, wt, wg, outl, fgl = pl.pallas_call(
        lambda *refs: gather_kernel(q, refs),
        out_shape=(
            struct((total, own), F32),
            struct((total, own), F32),
            struct((4, total, own), BF),
            struct((K, co, total), BF),
            struct((2, ci, co), F32),
            struct((ci, own), F32),
            struct((ci, own), F32),
        ),
        in_specs=[vmem] * (2 * q + 2),
        out_specs=(vmem,) * 7,
        scratch_shapes=[pltpu.VMEM((total, K * co), F32)],
        compiler_params=params,
        cost_estimate=pl.CostEstimate(flops=4 * total * own * own, bytes_accessed=4 << 20, transcendentals=0),
        name="gather",
    )(*packs, *tus, op, weights)

    x3, two, gh2 = pl.pallas_call(
        functools.partial(second_kernel, q),
        out_shape=(struct((n, 4 * ci, bw), BF), struct((2, total, own), BF), struct((2, ci, own), BF)),
        in_specs=[vmem] * 10,
        out_specs=(vmem,) * 3,
        scratch_shapes=[pltpu.VMEM((total, n * bw), BF), pltpu.VMEM((2 * ci, bw), F32)],
        compiler_params=params,
        name="second",
    )(y2, z2, marks, op, tpre, upre, full, wt, wg, weights)
    y3 = row_exchange(x3, n)

    output, feature_grad, weight_grad = pl.pallas_call(
        last_kernel,
        out_shape=(struct((ci, own), BF), struct((ci, own), BF), struct((K, ci, co), F32)),
        in_specs=[vmem] * 9,
        out_specs=(vmem,) * 3,
        scratch_shapes=[pltpu.VMEM((ci, wide), BF)],
        compiler_params=params,
        name="last",
    )(y3, marks, op, outl, fgl, two, gh2, wt, weights)
    return output, feature_grad, weight_grad


def solution(mesh):
    placed = (
        P("ch", "rows"),
        P("rows", None, None, None),
        P("rows", None),
        P("rows", None, None),
        P(None, "ch", None),
        P("ch", "rows"),
    )
    return jax.shard_map(
        body,
        mesh=mesh,
        in_specs=placed,
        out_specs=(P("ch", "rows"), P("ch", "rows"), P(None, "ch", None)),
        check_vma=False,
    )
```

```python
import functools

import jax
import jax.numpy as jnp
from jax import lax
from jax.experimental import pallas as pl
from jax.experimental.pallas import tpu as pltpu
from jax.sharding import PartitionSpec as P

K = 4
BF = jnp.bfloat16
F32 = jnp.float32
SMEM = pltpu.MemorySpace.SMEM
VMEM = pltpu.MemorySpace.VMEM


def nn(a, b):
    return lax.dot_general(a, b, (((1,), (0,)), ((), ())), preferred_element_type=F32)


def nt(a, b):
    return lax.dot_general(a, b, (((1,), (1,)), ((), ())), preferred_element_type=F32)


def lanes(index, width):
    return pl.ds(pl.multiple_of(index * width, width), width)


def turn(n):
    return 5 * n // 8


def member(device, n):
    return (turn(n) - device) % n


def row_exchange(value, n):
    order = [(turn(n) - i) % n for i in range(n)]
    return lax.all_to_all(value, "rows", 0, 0, axis_index_groups=[order])


def spread(device, pair, n, half):
    return (device * half + pair - turn(n) * half - 1) % (n * half)


def spread_exchange(value, n, q):
    half = q // 2
    groups = []
    for parity in range(2):
        members = [row * q + 2 * pair + parity for row in range(n) for pair in range(half)]
        start = turn(n) * half + 1
        groups.append(members[start:] + members[:start])
    return lax.all_to_all(value, ("rows", "ch"), 0, 0, axis_index_groups=groups)


def swap(value, q, bit):
    return lax.ppermute(value, "ch", [(i, i ^ bit) for i in range(q)])


def push_kernel(cols_h, needs_h, f_h, c_h, w_h, tiles, x1, pack, cols, needs, cells, where, f, c, w, buf, acc, sems):
    nb, tpr = cols.shape
    n, ci, bw = acc.shape
    small = [(cols_h, cols), (needs_h, needs), (f_h, f), (c_h, c), (w_h, w)]
    copies = [pltpu.make_async_copy(src, dst, sems.at[i]) for i, (src, dst) in enumerate(small)]
    for r in range(nb):
        copies.append(pltpu.make_async_copy(tiles.at[r], buf.at[pl.ds(r * tpr, tpr)], sems.at[len(small) + r]))
    for copy in copies:
        copy.start()
    for o in range(n):
        acc[o] = jnp.zeros((ci, bw), F32)
    copies[0].wait()
    count = jnp.int32(0)
    for r in range(nb):
        for t in range(1, tpr):
            v = cols[r, t]
            cells[count] = v - nb
            where[count] = r * tpr + t
            count = count + (v >= nb).astype(jnp.int32)
    for copy in copies[1:5]:
        copy.wait()
    for o in range(n):
        for b in range(nb):
            x1[member(o, n), b * ci : (b + 1) * ci, :] = f[:, b * bw : (b + 1) * bw]
        x1[member(o, n), (nb + 1) * ci :, :] = jnp.full((8, bw), needs[0, o].astype(F32)).astype(BF)
    pack[0:ci] = f[...]
    pack[ci : 2 * ci] = c[...]
    for k in range(K):
        width = w.shape[2]
        pack[2 * ci :, k * width : (k + 1) * width] = w[k]
    for copy in copies[5:]:
        copy.wait()

    def products(step, carry):
        for j in range(n):
            i = jnp.minimum(step * n + j, nb * tpr - 1)
            live = i < count
            o = jnp.where(live, cells[i], 0)
            at = jnp.where(live, where[i], 0)
            part = nn(c[:, lanes(at // tpr, bw)], buf[at])
            acc[o] += jnp.where(live, part, 0.0)
        return carry

    lax.fori_loop(0, (count + n - 1) // n, products, 0)
    for o in range(n):
        x1[member(o, n), nb * ci : (nb + 1) * ci, :] = acc[o].astype(BF)


def combine_kernel(cols, f, c, tiles, op, lf, ltc, total, buf, sems):
    nb, tpr = cols.shape
    bw = tiles.shape[2]
    own = f.shape[1]
    copies = [pltpu.make_async_copy(tiles.at[r], buf.at[r], sems.at[r]) for r in range(nb)]
    for copy in copies:
        copy.start()
    for r in range(nb):
        rows = slice(r * bw, (r + 1) * bw)
        total[...] = jnp.zeros_like(total)
        copies[r].wait()
        for t in range(tpr):
            at = lanes(cols[r, t], bw)
            total[:, at] += buf[r, t].astype(F32)
        op[rows, :] = total[...].astype(BF)
    local = op[:, :own]
    lf[...] = nt(f[...], local)
    ltc[...] = nn(c[...], local)


def first_kernel(needs, y1, op, lf, ltc, x2, tu, marks_ref, gh):
    n, rows, bw = y1.shape
    ci, own = lf.shape
    nb = own // bw
    half = x2.shape[0] // n
    for o in range(n):
        at = jnp.maximum(needs[0, o], 0) * ci
        gh[:, o * bw : (o + 1) * bw] = y1[member(o, n), pl.ds(pl.multiple_of(at, ci), ci), :]
    t1 = (lf[...] + nt(gh[...], op[:, own:])).astype(BF)
    marks = []
    for o in range(n):
        mark = y1[member(o, n), (nb + 1) * ci :, :].astype(F32)
        marks.append(jnp.concatenate([mark] * (ci // 8), axis=0))
        marks_ref[o] = marks[o].astype(BF)
    u1 = []
    for b in range(nb):
        u = ltc[:, b * bw : (b + 1) * bw]
        for o in range(n):
            u = u + jnp.where(marks[o] == b, y1[member(o, n), nb * ci : (nb + 1) * ci, :].astype(F32), 0.0)
        u1.append(u.astype(BF))
    for b in range(nb):
        tu[ci : 2 * ci, b * bw : (b + 1) * bw] = u1[b]
    sent = nn(tu[ci : 2 * ci], op[:, own:]).astype(BF)
    tu[0:ci] = t1
    tf = t1.astype(F32)
    for o in range(n):
        blk = jnp.zeros((ci, bw), F32)
        for b in range(nb):
            blk = jnp.where(marks[o] == b, tf[:, b * bw : (b + 1) * bw], blk)
        blk = blk.astype(BF)
        for s in range(half):
            x2[spread(o, s, n, half), 0:ci, :] = blk
            x2[spread(o, s, n, half), ci:, :] = sent[:, o * bw : (o + 1) * bw]


def gather_kernel(q, refs):
    packs = refs[:q]
    tus = refs[q : 2 * q]
    op, w, tpre, upre, full, wt, wg, outl, fgl, wbuf = refs[2 * q :]
    own = tpre.shape[1]
    total = tpre.shape[0]
    ci = total // q
    co = wt.shape[1]
    me = lax.axis_index("ch")
    for s in range(q):
        spot = pl.ds(pl.multiple_of((me ^ s) * ci, ci), ci)
        full[0, spot, :] = packs[s][0:ci, :]
        full[1, spot, :] = packs[s][ci : 2 * ci, :]
        full[2, spot, :] = tus[s][0:ci, :]
        full[3, spot, :] = tus[s][ci : 2 * ci, :]
        wbuf[spot, :] = packs[s][2 * ci :, : K * co].astype(F32)
    for k in range(K):
        turned = wbuf[:, k * co : (k + 1) * co].T
        wt[k] = turned.astype(BF)
    mine = pl.ds(pl.multiple_of(me * ci, ci), ci)
    outl[...] = nn(wt[0, mine, :], full[0]) + nn(wt[1, mine, :], full[2]) - nn(wt[3, mine, :], full[2])
    fgl[...] = nn(w[0], full[1]) + nn(w[1], full[3]) - nn(w[3], full[3])
    local = op[:, :own]
    tpre[...] = 2.0 * nt(full[2], local) - full[0].astype(F32)
    upre[...] = 2.0 * nn(full[3], local) - full[1].astype(F32)
    wg[0] = nt(packs[0][0:ci, :], full[1])
    wg[1] = nt(tus[0][0:ci, :], full[1])


def second_kernel(q, y2, z2, marks_ref, op, tpre, upre, full, wt, wg, w, x3, two, gh2, gh, low):
    n, ci, bw = marks_ref.shape
    total, own = tpre.shape
    nb = own // bw
    me = lax.axis_index("ch")
    mine = pl.ds(pl.multiple_of(me * ci, ci), ci)
    half = q // 2
    sources = []
    for s in range(half):
        own_at = 2 * s + me % 2
        sources.append((s, y2, pl.ds(pl.multiple_of(own_at * ci, ci), ci)))
        sources.append((s, z2, pl.ds(pl.multiple_of((own_at ^ 1) * ci, ci), ci)))
    for o in range(n):
        for s, came, spot in sources:
            gh[spot, o * bw : (o + 1) * bw] = came[spread(o, s, n, half), 0:ci, :]
    two[0] = (tpre[...] + 2.0 * nt(gh[...], op[:, own:])).astype(BF)
    marks = [marks_ref[o].astype(F32) for o in range(n)]
    for s, came, spot in sources:
        for b in range(nb):
            u = jnp.zeros((ci, bw), F32)
            for o in range(n):
                u = u + jnp.where(marks[o] == b, came[spread(o, s, n, half), ci:, :].astype(F32), 0.0)
            at = (spot, slice(b * bw, (b + 1) * bw))
            two[(1,) + at] = (upre[at] + 2.0 * u).astype(BF)
    g = nn(wt[K - 1, mine, :], two[0]).astype(BF)
    h = nn(w[K - 1], two[1]).astype(BF)
    gh2[0] = g
    gh2[1] = h
    sent = nn(h, op[:, own:]).astype(BF)
    t2 = two[0, mine, :]
    co = w.shape[2]
    wg2 = nt(t2, full[1])
    wg3 = 2.0 * nt(t2, full[3]) - wg[1]
    low[0:ci, 0:co] = wg[0]
    low[0:ci, co:] = wg[1]
    low[ci:, 0:co] = wg2
    low[ci:, co:] = wg3
    packed = low[...].astype(BF)
    gf = g.astype(F32)
    for o in range(n):
        blk = jnp.zeros((ci, bw), F32)
        for b in range(nb):
            blk = jnp.where(marks[o] == b, gf[:, b * bw : (b + 1) * bw], blk)
        x3[member(o, n), 0:ci, :] = blk.astype(BF)
        x3[member(o, n), ci : 2 * ci, :] = sent[:, o * bw : (o + 1) * bw]
        x3[member(o, n), 2 * ci :, :] = packed


def last_kernel(y3, marks_ref, op, outl, fgl, two, gh2, wt, w, out, fg, wgrad, gh):
    n, ci, bw = marks_ref.shape
    own = outl.shape[1]
    nb = own // bw
    co = wgrad.shape[2]
    me = lax.axis_index("ch")
    mine = pl.ds(pl.multiple_of(me * ci, ci), ci)
    gh[:, :own] = gh2[0]
    for o in range(n):
        gh[:, own + o * bw : own + (o + 1) * bw] = y3[member(o, n), 0:ci, :]
    out[...] = (outl[...] + nn(wt[2, mine, :], two[0]) + 2.0 * nt(gh[...], op[...])).astype(BF)
    back = nn(gh2[1], op[:, :own])
    base = fgl[...] + nn(w[2], two[1])
    for b in range(nb):
        spot = slice(b * bw, (b + 1) * bw)
        u = back[:, spot]
        for o in range(n):
            u = u + jnp.where(marks_ref[o].astype(F32) == b, y3[member(o, n), ci : 2 * ci, :].astype(F32), 0.0)
        fg[:, spot] = (base[:, spot] + 2.0 * u).astype(BF)
    wsum = y3[member(0, n), 2 * ci :, :].astype(F32)
    for o in range(1, n):
        wsum = wsum + y3[member(o, n), 2 * ci :, :].astype(F32)
    wgrad[0] = wsum[0:ci, 0:co]
    wgrad[1] = wsum[0:ci, co:]
    wgrad[2] = wsum[ci:, 0:co]
    wgrad[3] = wsum[ci:, co:]


def body(features, tiles, tile_cols, needs, weights, cotangent):
    ci, own = features.shape
    nb, tpr, bw, _ = tiles.shape
    co = weights.shape[2]
    n = lax.axis_size("rows")
    q = lax.axis_size("ch")
    total = ci * q
    cells = nb + n
    wide = cells * bw
    struct = jax.ShapeDtypeStruct
    smem = pl.BlockSpec(memory_space=SMEM)
    vmem = pl.BlockSpec(memory_space=VMEM)
    hbm = pl.BlockSpec(memory_space=pltpu.MemorySpace.HBM)
    limit = (16 << 20) + 4 * own * wide * 2
    params = pltpu.CompilerParams(vmem_limit_bytes=limit)
    packed = pltpu.CompilerParams(vmem_limit_bytes=62 << 20)

    needs = needs.reshape(1, n)
    x1, pack = pl.pallas_call(
        push_kernel,
        out_shape=(struct((n, (nb + 1) * ci + 8, bw), BF), struct((3 * ci, own), BF)),
        in_specs=[hbm] * 6,
        out_specs=(vmem, vmem),
        scratch_shapes=[
            pltpu.SMEM((nb, tpr), jnp.int32),
            pltpu.SMEM((1, n), jnp.int32),
            pltpu.SMEM((nb * tpr,), jnp.int32),
            pltpu.SMEM((nb * tpr,), jnp.int32),
            pltpu.VMEM((ci, own), BF),
            pltpu.VMEM((ci, own), BF),
            pltpu.VMEM((K, ci, co), BF),
            pltpu.VMEM((nb * tpr, bw, bw), BF),
            pltpu.VMEM((n, ci, bw), F32),
            pltpu.SemaphoreType.DMA((5 + nb,)),
        ],
        compiler_params=packed,
        name="push",
    )(tile_cols, needs, features, cotangent, weights, tiles)
    y1 = row_exchange(x1, n)

    op, lf, ltc = pl.pallas_call(
        combine_kernel,
        out_shape=(struct((own, wide), BF), struct((ci, own), F32), struct((ci, own), F32)),
        in_specs=[smem, vmem, vmem, hbm],
        out_specs=(vmem,) * 3,
        scratch_shapes=[
            pltpu.VMEM((bw, wide), F32),
            pltpu.VMEM((nb, tpr, bw, bw), BF),
            pltpu.SemaphoreType.DMA((nb,)),
        ],
        compiler_params=pltpu.CompilerParams(vmem_limit_bytes=51 << 20),
        cost_estimate=pl.CostEstimate(flops=4 * ci * own * own, bytes_accessed=8 << 20, transcendentals=0),
        name="combine",
    )(tile_cols, features, cotangent, tiles)

    packs = [pack, swap(pack, q, 1), swap(pack, q, 2), swap(pack, q, 3)]
    y1, *packs[1:] = lax.optimization_barrier((y1, *packs[1:]))

    x2, tu, marks = pl.pallas_call(
        first_kernel,
        out_shape=(struct((n * (q // 2), 2 * ci, bw), BF), struct((2 * ci, own), BF), struct((n, ci, bw), BF)),
        in_specs=[smem] + [vmem] * 4,
        out_specs=(vmem,) * 3,
        scratch_shapes=[pltpu.VMEM((ci, n * bw), BF)],
        compiler_params=params,
        name="first",
    )(needs, y1, op, lf, ltc)
    y2 = spread_exchange(x2, n, q)
    tus = [tu, swap(tu, q, 1), swap(tu, q, 2)]
    tus.append(swap(tu, q, 3))
    y2, *tus[1:] = lax.optimization_barrier((y2, *tus[1:]))
    z2 = swap(y2, q, 1)

    tpre, upre, full, wt, wg, outl, fgl = pl.pallas_call(
        lambda *refs: gather_kernel(q, refs),
        out_shape=(
            struct((total, own), F32),
            struct((total, own), F32),
            struct((4, total, own), BF),
            struct((K, co, total), BF),
            struct((2, ci, co), F32),
            struct((ci, own), F32),
            struct((ci, own), F32),
        ),
        in_specs=[vmem] * (2 * q + 2),
        out_specs=(vmem,) * 7,
        scratch_shapes=[pltpu.VMEM((total, K * co), F32)],
        compiler_params=params,
        cost_estimate=pl.CostEstimate(flops=4 * total * own * own, bytes_accessed=4 << 20, transcendentals=0),
        name="gather",
    )(*packs, *tus, op, weights)

    x3, two, gh2 = pl.pallas_call(
        functools.partial(second_kernel, q),
        out_shape=(struct((n, 4 * ci, bw), BF), struct((2, total, own), BF), struct((2, ci, own), BF)),
        in_specs=[vmem] * 10,
        out_specs=(vmem,) * 3,
        scratch_shapes=[pltpu.VMEM((total, n * bw), BF), pltpu.VMEM((2 * ci, bw), F32)],
        compiler_params=params,
        name="second",
    )(y2, z2, marks, op, tpre, upre, full, wt, wg, weights)
    y3 = row_exchange(x3, n)

    output, feature_grad, weight_grad = pl.pallas_call(
        last_kernel,
        out_shape=(struct((ci, own), BF), struct((ci, own), BF), struct((K, ci, co), F32)),
        in_specs=[vmem] * 9,
        out_specs=(vmem,) * 3,
        scratch_shapes=[pltpu.VMEM((ci, wide), BF)],
        compiler_params=params,
        name="last",
    )(y3, marks, op, outl, fgl, two, gh2, wt, weights)
    return output, feature_grad, weight_grad


def solution(mesh):
    placed = (
        P("ch", "rows"),
        P("rows", None, None, None),
        P("rows", None),
        P("rows", None, None),
        P(None, "ch", None),
        P("ch", "rows"),
    )
    return jax.shard_map(
        body,
        mesh=mesh,
        in_specs=placed,
        out_specs=(P("ch", "rows"), P("ch", "rows"), P(None, "ch", None)),
        check_vma=False,
    )
```

```python
import functools

import jax
import jax.numpy as jnp
from jax import lax
from jax.experimental import pallas as pl
from jax.experimental.pallas import tpu as pltpu
from jax.sharding import PartitionSpec as P

K = 4
BF = jnp.bfloat16
F32 = jnp.float32
SMEM = pltpu.MemorySpace.SMEM
VMEM = pltpu.MemorySpace.VMEM


def nn(a, b):
    return lax.dot_general(a, b, (((1,), (0,)), ((), ())), preferred_element_type=F32)


def nt(a, b):
    return lax.dot_general(a, b, (((1,), (1,)), ((), ())), preferred_element_type=F32)


def lanes(index, width):
    return pl.ds(pl.multiple_of(index * width, width), width)


def turn(n):
    return 5 * n // 8


def member(device, n):
    return (turn(n) - device) % n


def row_exchange(value, n):
    order = [(turn(n) - i) % n for i in range(n)]
    return lax.all_to_all(value, "rows", 0, 0, axis_index_groups=[order])


def spread(device, pair, n, half):
    return (turn(n) * half - 1 - device * half - pair) % (n * half)


def spread_exchange(value, n, q):
    half = q // 2
    groups = []
    for parity in range(2):
        members = [row * q + 2 * pair + parity for row in range(n) for pair in range(half)]
        start = turn(n) * half - 1
        groups.append([members[(start - i) % len(members)] for i in range(len(members))])
    return lax.all_to_all(value, ("rows", "ch"), 0, 0, axis_index_groups=groups)


def swap(value, q, bit):
    return lax.ppermute(value, "ch", [(i, i ^ bit) for i in range(q)])


def push_kernel(cols_h, needs_h, f_h, c_h, w_h, tiles, x1, pack, cols, needs, cells, where, f, c, w, buf, acc, sems):
    nb, tpr = cols.shape
    n, ci, bw = acc.shape
    small = [(cols_h, cols), (needs_h, needs), (f_h, f), (c_h, c), (w_h, w)]
    copies = [pltpu.make_async_copy(src, dst, sems.at[i]) for i, (src, dst) in enumerate(small)]
    for r in range(nb):
        copies.append(pltpu.make_async_copy(tiles.at[r], buf.at[pl.ds(r * tpr, tpr)], sems.at[len(small) + r]))
    for copy in copies:
        copy.start()
    for o in range(n):
        acc[o] = jnp.zeros((ci, bw), F32)
    copies[0].wait()
    count = jnp.int32(0)
    for r in range(nb):
        for t in range(1, tpr):
            v = cols[r, t]
            cells[count] = v - nb
            where[count] = r * tpr + t
            count = count + (v >= nb).astype(jnp.int32)
    for copy in copies[1:5]:
        copy.wait()
    for o in range(n):
        for b in range(nb):
            x1[member(o, n), b * ci : (b + 1) * ci, :] = f[:, b * bw : (b + 1) * bw]
        x1[member(o, n), (nb + 1) * ci :, :] = jnp.full((8, bw), needs[0, o].astype(F32)).astype(BF)
    pack[0:ci] = f[...]
    pack[ci : 2 * ci] = c[...]
    for k in range(K):
        width = w.shape[2]
        pack[2 * ci :, k * width : (k + 1) * width] = w[k]
    for copy in copies[5:]:
        copy.wait()

    def products(step, carry):
        for j in range(n):
            i = jnp.minimum(step * n + j, nb * tpr - 1)
            live = i < count
            o = jnp.where(live, cells[i], 0)
            at = jnp.where(live, where[i], 0)
            part = nn(c[:, lanes(at // tpr, bw)], buf[at])
            acc[o] += jnp.where(live, part, 0.0)
        return carry

    lax.fori_loop(0, (count + n - 1) // n, products, 0)
    for o in range(n):
        x1[member(o, n), nb * ci : (nb + 1) * ci, :] = acc[o].astype(BF)


def combine_kernel(cols, f, c, tiles, op, lf, ltc, total, buf, sems):
    nb, tpr = cols.shape
    bw = tiles.shape[2]
    own = f.shape[1]
    copies = [pltpu.make_async_copy(tiles.at[r], buf.at[r], sems.at[r]) for r in range(nb)]
    for copy in copies:
        copy.start()
    for r in range(nb):
        rows = slice(r * bw, (r + 1) * bw)
        total[...] = jnp.zeros_like(total)
        copies[r].wait()
        for t in range(tpr):
            at = lanes(cols[r, t], bw)
            total[:, at] += buf[r, t].astype(F32)
        op[rows, :] = total[...].astype(BF)
    local = op[:, :own]
    lf[...] = nt(f[...], local)
    ltc[...] = nn(c[...], local)


def first_kernel(needs, y1, op, lf, ltc, x2, tu, marks_ref, gh):
    n, rows, bw = y1.shape
    ci, own = lf.shape
    nb = own // bw
    half = x2.shape[0] // n
    for o in range(n):
        at = jnp.maximum(needs[0, o], 0) * ci
        gh[:, o * bw : (o + 1) * bw] = y1[member(o, n), pl.ds(pl.multiple_of(at, ci), ci), :]
    t1 = (lf[...] + nt(gh[...], op[:, own:])).astype(BF)
    marks = []
    for o in range(n):
        mark = y1[member(o, n), (nb + 1) * ci :, :].astype(F32)
        marks.append(jnp.concatenate([mark] * (ci // 8), axis=0))
        marks_ref[o] = marks[o].astype(BF)
    u1 = []
    for b in range(nb):
        u = ltc[:, b * bw : (b + 1) * bw]
        for o in range(n):
            u = u + jnp.where(marks[o] == b, y1[member(o, n), nb * ci : (nb + 1) * ci, :].astype(F32), 0.0)
        u1.append(u.astype(BF))
    for b in range(nb):
        tu[ci : 2 * ci, b * bw : (b + 1) * bw] = u1[b]
    sent = nn(tu[ci : 2 * ci], op[:, own:]).astype(BF)
    tu[0:ci] = t1
    tf = t1.astype(F32)
    for o in range(n):
        blk = jnp.zeros((ci, bw), F32)
        for b in range(nb):
            blk = jnp.where(marks[o] == b, tf[:, b * bw : (b + 1) * bw], blk)
        blk = blk.astype(BF)
        for s in range(half):
            x2[spread(o, s, n, half), 0:ci, :] = blk
            x2[spread(o, s, n, half), ci:, :] = sent[:, o * bw : (o + 1) * bw]


def gather_kernel(q, refs):
    packs = refs[:q]
    tus = refs[q : 2 * q]
    op, w, tpre, upre, full, wt, wg, outl, fgl, wbuf = refs[2 * q :]
    own = tpre.shape[1]
    total = tpre.shape[0]
    ci = total // q
    co = wt.shape[1]
    me = lax.axis_index("ch")
    for s in range(q):
        spot = pl.ds(pl.multiple_of((me ^ s) * ci, ci), ci)
        full[0, spot, :] = packs[s][0:ci, :]
        full[1, spot, :] = packs[s][ci : 2 * ci, :]
        full[2, spot, :] = tus[s][0:ci, :]
        full[3, spot, :] = tus[s][ci : 2 * ci, :]
        wbuf[spot, :] = packs[s][2 * ci :, : K * co].astype(F32)
    for k in range(K):
        turned = wbuf[:, k * co : (k + 1) * co].T
        wt[k] = turned.astype(BF)
    mine = pl.ds(pl.multiple_of(me * ci, ci), ci)
    outl[...] = nn(wt[0, mine, :], full[0]) + nn(wt[1, mine, :], full[2]) - nn(wt[3, mine, :], full[2])
    fgl[...] = nn(w[0], full[1]) + nn(w[1], full[3]) - nn(w[3], full[3])
    local = op[:, :own]
    tpre[...] = 2.0 * nt(full[2], local) - full[0].astype(F32)
    upre[...] = 2.0 * nn(full[3], local) - full[1].astype(F32)
    wg[0] = nt(packs[0][0:ci, :], full[1])
    wg[1] = nt(tus[0][0:ci, :], full[1])


def second_kernel(q, y2, z2, marks_ref, op, tpre, upre, full, wt, wg, w, x3, two, gh2, gh, low):
    n, ci, bw = marks_ref.shape
    total, own = tpre.shape
    nb = own // bw
    me = lax.axis_index("ch")
    mine = pl.ds(pl.multiple_of(me * ci, ci), ci)
    half = q // 2
    sources = []
    for s in range(half):
        own_at = 2 * s + me % 2
        sources.append((s, y2, pl.ds(pl.multiple_of(own_at * ci, ci), ci)))
        sources.append((s, z2, pl.ds(pl.multiple_of((own_at ^ 1) * ci, ci), ci)))
    for o in range(n):
        for s, came, spot in sources:
            gh[spot, o * bw : (o + 1) * bw] = came[spread(o, s, n, half), 0:ci, :]
    two[0] = (tpre[...] + 2.0 * nt(gh[...], op[:, own:])).astype(BF)
    marks = [marks_ref[o].astype(F32) for o in range(n)]
    for s, came, spot in sources:
        for b in range(nb):
            u = jnp.zeros((ci, bw), F32)
            for o in range(n):
                u = u + jnp.where(marks[o] == b, came[spread(o, s, n, half), ci:, :].astype(F32), 0.0)
            at = (spot, slice(b * bw, (b + 1) * bw))
            two[(1,) + at] = (upre[at] + 2.0 * u).astype(BF)
    g = nn(wt[K - 1, mine, :], two[0]).astype(BF)
    h = nn(w[K - 1], two[1]).astype(BF)
    gh2[0] = g
    gh2[1] = h
    sent = nn(h, op[:, own:]).astype(BF)
    t2 = two[0, mine, :]
    co = w.shape[2]
    wg2 = nt(t2, full[1])
    wg3 = 2.0 * nt(t2, full[3]) - wg[1]
    low[0:ci, 0:co] = wg[0]
    low[0:ci, co:] = wg[1]
    low[ci:, 0:co] = wg2
    low[ci:, co:] = wg3
    packed = low[...].astype(BF)
    gf = g.astype(F32)
    for o in range(n):
        blk = jnp.zeros((ci, bw), F32)
        for b in range(nb):
            blk = jnp.where(marks[o] == b, gf[:, b * bw : (b + 1) * bw], blk)
        x3[member(o, n), 0:ci, :] = blk.astype(BF)
        x3[member(o, n), ci : 2 * ci, :] = sent[:, o * bw : (o + 1) * bw]
        x3[member(o, n), 2 * ci :, :] = packed


def last_kernel(y3, marks_ref, op, outl, fgl, two, gh2, wt, w, out, fg, wgrad, gh):
    n, ci, bw = marks_ref.shape
    own = outl.shape[1]
    nb = own // bw
    co = wgrad.shape[2]
    me = lax.axis_index("ch")
    mine = pl.ds(pl.multiple_of(me * ci, ci), ci)
    gh[:, :own] = gh2[0]
    for o in range(n):
        gh[:, own + o * bw : own + (o + 1) * bw] = y3[member(o, n), 0:ci, :]
    out[...] = (outl[...] + nn(wt[2, mine, :], two[0]) + 2.0 * nt(gh[...], op[...])).astype(BF)
    back = nn(gh2[1], op[:, :own])
    base = fgl[...] + nn(w[2], two[1])
    for b in range(nb):
        spot = slice(b * bw, (b + 1) * bw)
        u = back[:, spot]
        for o in range(n):
            u = u + jnp.where(marks_ref[o].astype(F32) == b, y3[member(o, n), ci : 2 * ci, :].astype(F32), 0.0)
        fg[:, spot] = (base[:, spot] + 2.0 * u).astype(BF)
    wsum = y3[member(0, n), 2 * ci :, :].astype(F32)
    for o in range(1, n):
        wsum = wsum + y3[member(o, n), 2 * ci :, :].astype(F32)
    wgrad[0] = wsum[0:ci, 0:co]
    wgrad[1] = wsum[0:ci, co:]
    wgrad[2] = wsum[ci:, 0:co]
    wgrad[3] = wsum[ci:, co:]


def body(features, tiles, tile_cols, needs, weights, cotangent):
    ci, own = features.shape
    nb, tpr, bw, _ = tiles.shape
    co = weights.shape[2]
    n = lax.axis_size("rows")
    q = lax.axis_size("ch")
    total = ci * q
    cells = nb + n
    wide = cells * bw
    struct = jax.ShapeDtypeStruct
    smem = pl.BlockSpec(memory_space=SMEM)
    vmem = pl.BlockSpec(memory_space=VMEM)
    hbm = pl.BlockSpec(memory_space=pltpu.MemorySpace.HBM)
    limit = (16 << 20) + 4 * own * wide * 2
    params = pltpu.CompilerParams(vmem_limit_bytes=limit)
    packed = pltpu.CompilerParams(vmem_limit_bytes=62 << 20)

    needs = needs.reshape(1, n)
    x1, pack = pl.pallas_call(
        push_kernel,
        out_shape=(struct((n, (nb + 1) * ci + 8, bw), BF), struct((3 * ci, own), BF)),
        in_specs=[hbm] * 6,
        out_specs=(vmem, vmem),
        scratch_shapes=[
            pltpu.SMEM((nb, tpr), jnp.int32),
            pltpu.SMEM((1, n), jnp.int32),
            pltpu.SMEM((nb * tpr,), jnp.int32),
            pltpu.SMEM((nb * tpr,), jnp.int32),
            pltpu.VMEM((ci, own), BF),
            pltpu.VMEM((ci, own), BF),
            pltpu.VMEM((K, ci, co), BF),
            pltpu.VMEM((nb * tpr, bw, bw), BF),
            pltpu.VMEM((n, ci, bw), F32),
            pltpu.SemaphoreType.DMA((5 + nb,)),
        ],
        compiler_params=packed,
        name="push",
    )(tile_cols, needs, features, cotangent, weights, tiles)
    y1 = row_exchange(x1, n)

    op, lf, ltc = pl.pallas_call(
        combine_kernel,
        out_shape=(struct((own, wide), BF), struct((ci, own), F32), struct((ci, own), F32)),
        in_specs=[smem, vmem, vmem, hbm],
        out_specs=(vmem,) * 3,
        scratch_shapes=[
            pltpu.VMEM((bw, wide), F32),
            pltpu.VMEM((nb, tpr, bw, bw), BF),
            pltpu.SemaphoreType.DMA((nb,)),
        ],
        compiler_params=pltpu.CompilerParams(vmem_limit_bytes=51 << 20),
        cost_estimate=pl.CostEstimate(flops=4 * ci * own * own, bytes_accessed=8 << 20, transcendentals=0),
        name="combine",
    )(tile_cols, features, cotangent, tiles)

    packs = [pack, swap(pack, q, 1), swap(pack, q, 2), swap(pack, q, 3)]
    y1, *packs[1:] = lax.optimization_barrier((y1, *packs[1:]))

    x2, tu, marks = pl.pallas_call(
        first_kernel,
        out_shape=(struct((n * (q // 2), 2 * ci, bw), BF), struct((2 * ci, own), BF), struct((n, ci, bw), BF)),
        in_specs=[smem] + [vmem] * 4,
        out_specs=(vmem,) * 3,
        scratch_shapes=[pltpu.VMEM((ci, n * bw), BF)],
        compiler_params=params,
        name="first",
    )(needs, y1, op, lf, ltc)
    y2 = spread_exchange(x2, n, q)
    tus = [tu, swap(tu, q, 1), swap(tu, q, 2)]
    tus.append(swap(tu, q, 3))
    y2, *tus[1:] = lax.optimization_barrier((y2, *tus[1:]))
    z2 = swap(y2, q, 1)

    tpre, upre, full, wt, wg, outl, fgl = pl.pallas_call(
        lambda *refs: gather_kernel(q, refs),
        out_shape=(
            struct((total, own), F32),
            struct((total, own), F32),
            struct((4, total, own), BF),
            struct((K, co, total), BF),
            struct((2, ci, co), F32),
            struct((ci, own), F32),
            struct((ci, own), F32),
        ),
        in_specs=[vmem] * (2 * q + 2),
        out_specs=(vmem,) * 7,
        scratch_shapes=[pltpu.VMEM((total, K * co), F32)],
        compiler_params=params,
        cost_estimate=pl.CostEstimate(flops=4 * total * own * own, bytes_accessed=4 << 20, transcendentals=0),
        name="gather",
    )(*packs, *tus, op, weights)

    x3, two, gh2 = pl.pallas_call(
        functools.partial(second_kernel, q),
        out_shape=(struct((n, 4 * ci, bw), BF), struct((2, total, own), BF), struct((2, ci, own), BF)),
        in_specs=[vmem] * 10,
        out_specs=(vmem,) * 3,
        scratch_shapes=[pltpu.VMEM((total, n * bw), BF), pltpu.VMEM((2 * ci, bw), F32)],
        compiler_params=params,
        name="second",
    )(y2, z2, marks, op, tpre, upre, full, wt, wg, weights)
    y3 = row_exchange(x3, n)

    output, feature_grad, weight_grad = pl.pallas_call(
        last_kernel,
        out_shape=(struct((ci, own), BF), struct((ci, own), BF), struct((K, ci, co), F32)),
        in_specs=[vmem] * 9,
        out_specs=(vmem,) * 3,
        scratch_shapes=[pltpu.VMEM((ci, wide), BF)],
        compiler_params=params,
        name="last",
    )(y3, marks, op, outl, fgl, two, gh2, wt, weights)
    return output, feature_grad, weight_grad


def solution(mesh):
    placed = (
        P("ch", "rows"),
        P("rows", None, None, None),
        P("rows", None),
        P("rows", None, None),
        P(None, "ch", None),
        P("ch", "rows"),
    )
    return jax.shard_map(
        body,
        mesh=mesh,
        in_specs=placed,
        out_specs=(P("ch", "rows"), P("ch", "rows"), P(None, "ch", None)),
        check_vma=False,
    )
```
